32 devices in a mesh: groups: 2 (over x), dates: 16 (over z, y, core).
Axes of the slice: x: 2, y: 2, z: 4, core: 2. Of those that a mesh axis runs over, the one named last changes fastest.
Arguments:
- scenes: bfloat16 [64, 4, 64, 128], P(('groups', 'dates')), parts along dimension 0, may hold values from -10 to 14
- cloud_mask: int32 [64, 64, 128], P(('groups', 'dates')), parts along dimension 0, may hold values 0 or 1
- region: int32 [128, 128], P('groups'), parts along dimension 0, may hold values from 0 to 7
Outputs:
- smoothed: bfloat16 [64, 4, 64, 128], P('groups', None, 'dates'), parts along dimension 0
- similarity: float32 [64, 32], P(('groups', 'dates')), parts along dimension 0
The draws below stay inside these ranges and needn't reach their ends.
There are 2 independent parts, one for each index of `groups`. The reference program is written for one: setup_inputs(seed, part) draws one part's arguments, and reference() takes and returns one part's arrays. A program takes and returns all parts, laid end to end along the dimension named above; each array names one. Nothing has to cross between parts.
All inputs are finite; a program needn't handle non-finite values. No bound on the sum of `cloud_mask` on one device may be relied on, other than what follows from the above.
Results may differ from the reference program's by a relative error of at most 0.0065.
Values may be sent and summed in bfloat16 or wider, within the bound.
No kernel may reach another device: no remote copies, remote signals or barrier semaphores. Data moves between devices by JAX's collectives and lax.ppermute only.
A program may use at most 64 MiB of HBM per device.

```python
import jax
import jax.numpy as jnp
from jax import lax

BANDS = 4
COLS = 128
REGIONS = 8
STEPS = 4
DATES = 32
ROWS = 64


def region_map(key):
    return jax.random.randint(jax.random.fold_in(key, 7), (ROWS, COLS), 0, REGIONS).astype(jnp.int32)


def draw_region(key, part):
    return region_map(key)


def draw_scenes(key, part):
    labels = region_map(key)
    offsets = jax.random.uniform(jax.random.fold_in(key, 11), (DATES, BANDS, REGIONS), jnp.float32, 0.5, 3.0)
    base = offsets[:, :, labels]
    noise = jax.random.truncated_normal(jax.random.fold_in(key, 13), -4.0, 4.0, (DATES, BANDS, ROWS, COLS), jnp.float32)
    return (base + noise).astype(jnp.bfloat16)


def plant(result, own_key, low, largest):
    extent = result.shape
    spot = [jax.random.randint(jax.random.fold_in(own_key, axis), (), 0, extent[axis]) for axis in range(len(extent))]
    result = result.at[tuple(spot)].set(low)
    longest = extent.index(max(extent))
    spot[longest] = (spot[longest] + 1) % extent[longest]
    return result.at[tuple(spot)].set(largest)


def setup_inputs(seed: int = 0, part: int = 0) -> dict:
    arg_keys = jax.random.split(jax.random.key(seed), 4)
    part_splits = jax.random.split(jax.random.fold_in(arg_keys[3], part), 4)
    scenes = draw_scenes(jax.random.fold_in(jax.random.fold_in(arg_keys[3], part), 71), part)
    cloud_mask = plant((jax.random.randint(part_splits[1], (DATES, ROWS, COLS), 0, 4) < 3).astype(jnp.int32), jax.random.fold_in(part_splits[1], 1), 0, 1)
    region = draw_region(jax.random.fold_in(jax.random.fold_in(arg_keys[3], part), 71), part)
    return {"scenes": scenes, "cloud_mask": cloud_mask, "region": region}


lam_space = 0.2
lam_time = 0.08


def edge_flux(difference):
    return difference / (1.0 + difference * difference)


def reference(scenes, cloud_mask, region):
    clear = cloud_mask.astype(jnp.float32)
    labels = jnp.arange(REGIONS, dtype=jnp.int32)[:, None, None]
    onehot = (region[None] == labels).astype(jnp.float32)
    counts = jnp.einsum("drc,grc->dg", clear, onehot)
    land_padded = jnp.pad((region > 0).astype(jnp.float32), 1)
    row_weight = land_padded[1:, 1:-1] * land_padded[:-1, 1:-1]
    col_weight = land_padded[1:-1, 1:] * land_padded[1:-1, :-1]
    edges = jnp.arange(DATES + 1, dtype=jnp.int32)
    date_weight = ((edges > 0) & (edges < DATES)).astype(jnp.float32)

    def one_band(band_values):
        values = band_values.astype(jnp.float32)
        sums = jnp.einsum("drc,grc->dg", values * clear, onehot)
        means = sums / (counts + 1.0)
        anomaly = (clear * (values - means[:, region])).astype(jnp.bfloat16)
        current = anomaly.astype(jnp.float32)
        for step_index in range(STEPS):
            padded_rows = jnp.pad(current, ((0, 0), (1, 1), (0, 0)))
            row_flux = lam_space * row_weight * edge_flux(padded_rows[:, 1:] - padded_rows[:, :-1])
            padded_cols = jnp.pad(current, ((0, 0), (0, 0), (1, 1)))
            col_flux = lam_space * col_weight * edge_flux(padded_cols[:, :, 1:] - padded_cols[:, :, :-1])
            padded_dates = jnp.pad(current, ((1, 1), (0, 0), (0, 0)))
            date_flux = lam_time * date_weight[:, None, None] * edge_flux(padded_dates[1:] - padded_dates[:-1])
            current = current + (row_flux[:, 1:] - row_flux[:, :-1]) + (col_flux[:, :, 1:] - col_flux[:, :, :-1]) + (date_flux[1:] - date_flux[:-1])
        return current.astype(jnp.bfloat16)

    smoothed = jnp.moveaxis(lax.map(one_band, jnp.moveaxis(scenes, 1, 0)), 0, 1)
    flat = smoothed.reshape(DATES, -1).astype(jnp.float32)
    similarity = jnp.dot(flat, flat.T, precision=lax.Precision.HIGHEST, preferred_element_type=jnp.float32) / (BANDS * ROWS * COLS)
    return smoothed, similarity
```

```python
import functools

import jax
import jax.numpy as jnp
from jax import lax
from jax.experimental import pallas as pl
from jax.experimental.pallas import tpu as pltpu
from jax.sharding import PartitionSpec as P

REGIONS = 8
STEPS = 4
HALO = 8
SHARED = 2

lam_space = 0.2
lam_time = 0.08

LIMIT = 48 * 1024 * 1024


def phi(difference):
    return difference / (1.0 + difference * difference)


class Plan:
    def __init__(self, devices, bands, rows):
        self.devices, self.bands, self.rows = devices, bands, rows
        planes = devices // bands
        self.shared = min(SHARED, planes)
        self.slabs = planes // self.shared
        self.plane_rows = rows // planes
        self.own_rows = rows // devices
        self.slab_rows = rows // self.slabs
        margin = HALO * min(self.slabs - 1, 2)
        self.window = self.slab_rows + margin

    def slab(self, index):
        return index // (self.bands * self.shared)

    def start(self, index):
        first = self.slab(index) * self.slab_rows - HALO
        last = self.rows - self.window
        if isinstance(index, int):
            return min(max(first, 0), last)
        return jnp.clip(first, 0, last)


def anomaly_kernel(plan, scenes_ref, mask_ref, region_ref, send_ref, sums_ref):
    date_dev, bands, rows, cols = scenes_ref.shape
    tiles = rows // 8
    per_region = bands + 1

    def tile_rows(i):
        return pl.ds(pl.multiple_of(i * 8, 8), 8)

    for date in range(date_dev):

        def gather(i, sums):
            clear = mask_ref[date, tile_rows(i)] > 0
            label = jnp.where(clear, region_ref[tile_rows(i)], -1)
            values = [scenes_ref[date, band, tile_rows(i)].astype(jnp.float32) for band in range(bands)]
            out = []
            for g in range(REGIONS):
                here = label == g
                for band in range(bands):
                    out.append(sums[g * per_region + band] + jnp.where(here, values[band], 0.0))
                out.append(sums[g * per_region + bands] + jnp.where(here, 1.0, 0.0))
            return tuple(out)

        zero = jnp.zeros((8, cols), jnp.float32)
        sums = lax.fori_loop(0, tiles, gather, (zero,) * (REGIONS * per_region), unroll=min(tiles, 8))
        for i, total in enumerate(sums):
            sums_ref[date, i : i + 1] = jnp.sum(total, axis=0, keepdims=True)

    means = []
    for date in range(date_dev):
        totals = jnp.sum(sums_ref[date], axis=1, keepdims=True)
        for band in range(bands):
            means.append(
                [
                    totals[g * per_region + band : g * per_region + band + 1]
                    / (totals[g * per_region + bands : g * per_region + bands + 1] + 1.0)
                    for g in range(REGIONS)
                ]
            )

    region = region_ref[...]
    for date in range(date_dev):
        clear = mask_ref[date].astype(jnp.float32)
        for band in range(bands):
            mean = jnp.zeros((rows, cols), jnp.float32)
            for g in range(REGIONS):
                mean = jnp.where(region == g, jnp.broadcast_to(means[date * bands + band][g], (rows, cols)), mean)
            anomaly = (clear * (scenes_ref[date, band].astype(jnp.float32) - mean)).astype(jnp.bfloat16)
            for target in range(band, plan.devices, bands):
                first = plan.start(target)
                send_ref[target, date] = anomaly[first : first + plan.window]


def diffuse_kernel(plan, dates, got_ref, region_ref, stay_ref, send_ref, gram_ref, field_ref):
    window, cols = plan.window, got_ref.shape[-1]
    me = lax.axis_index("dates")
    start = plan.start(me)
    land = (region_ref[pl.ds(pl.multiple_of(start, 8), window)] > 0).astype(jnp.float32)
    row = lax.broadcasted_iota(jnp.int32, (window, cols), 0)
    col = lax.broadcasted_iota(jnp.int32, (window, cols), 1)
    down = jnp.where(row < window - 1, pltpu.roll(land, window - 1, 0), 0.0)
    right = jnp.where(col < cols - 1, pltpu.roll(land, cols - 1, 1), 0.0)
    row_weight = lam_space * land * down
    col_weight = lam_space * land * right

    def at(t):
        return pl.ds(pl.multiple_of(t * window, 8), window)

    def load_first(t):
        return got_ref[t].astype(jnp.float32)

    def load(t):
        return field_ref[at(t)]

    for step in range(STEPS):
        read = load_first if step == 0 else load

        def advance(current, following, date_in):
            row_flux = row_weight * phi(pltpu.roll(current, window - 1, 0) - current)
            col_flux = col_weight * phi(pltpu.roll(current, cols - 1, 1) - current)
            date_out = jnp.zeros_like(current) if following is None else lam_time * phi(following - current)
            new = (
                current
                + (row_flux - pltpu.roll(row_flux, 1, 0))
                + (col_flux - pltpu.roll(col_flux, 1, 1))
                + (date_out - date_in)
            )
            return new, date_out

        def one(t, carry):
            current, date_in = carry
            following = read(t + 1)
            new, date_out = advance(current, following, date_in)
            field_ref[at(t)] = new
            return following, date_out

        last, date_in = lax.fori_loop(
            0, dates - 1, one, (read(0), jnp.zeros((window, cols), jnp.float32)), unroll=1
        )
        new, _ = advance(last, None, date_in)
        field_ref[at(dates - 1)] = new

    half = plan.plane_rows // 2
    pair = (me // 2) % 2
    plane_first = (me // plan.bands) * plan.plane_rows - start
    stay_first = pl.multiple_of(plane_first + pair * half, 8)
    send_first = pl.multiple_of(plane_first + (1 - pair) * half, 8)
    for t in range(dates):
        stay_ref[t] = field_ref[pl.ds(t * window + stay_first, half)].astype(jnp.bfloat16)
        send_ref[t] = field_ref[pl.ds(t * window + send_first, half)].astype(jnp.bfloat16)

    slab_first = plan.slab(me) * plan.slab_rows - start

    def gram(i, total):
        rows = jnp.concatenate(
            [field_ref[pl.ds(slab_first + 2 * i + j, dates, stride=window)] for j in range(2)], axis=1
        ).astype(jnp.bfloat16)
        return total + lax.dot_general(
            rows, rows, (((1,), (1,)), ((), ())), preferred_element_type=jnp.float32
        )

    gram_ref[...] = lax.fori_loop(
        0, plan.slab_rows // 2, gram, jnp.zeros((dates, dates), jnp.float32), unroll=min(8, plan.slab_rows // 2)
    )


def swap(x, bit):
    count = lax.axis_size("dates")
    return lax.ppermute(x, "dates", [(i, i ^ bit) for i in range(count)])


def local(scenes, cloud_mask, region):
    date_dev, bands, rows, cols = scenes.shape
    devices = lax.axis_size("dates")
    dates = date_dev * devices
    plan = Plan(devices, bands, rows)
    me = lax.axis_index("dates")
    vmem = pl.BlockSpec(memory_space=pltpu.VMEM)
    params = pltpu.CompilerParams(vmem_limit_bytes=LIMIT)

    send = pl.pallas_call(
        functools.partial(anomaly_kernel, plan),
        out_shape=jax.ShapeDtypeStruct((devices, date_dev, plan.window, cols), jnp.bfloat16),
        in_specs=[vmem] * 3,
        out_specs=vmem,
        scratch_shapes=[pltpu.VMEM((date_dev, REGIONS * (bands + 1), cols), jnp.float32)],
        compiler_params=params,
    )(scenes, cloud_mask, region)
    got = lax.all_to_all(send, "dates", split_axis=0, concat_axis=0, tiled=True)
    half = plan.plane_rows // 2
    stay, away, gram = pl.pallas_call(
        functools.partial(diffuse_kernel, plan, dates),
        out_shape=(
            jax.ShapeDtypeStruct((dates, half, cols), jnp.bfloat16),
            jax.ShapeDtypeStruct((dates, half, cols), jnp.bfloat16),
            jax.ShapeDtypeStruct((dates, dates), jnp.float32),
        ),
        in_specs=[vmem] * 2,
        out_specs=(vmem,) * 3,
        scratch_shapes=[pltpu.VMEM((dates * plan.window, cols), jnp.float32)],
        compiler_params=params,
    )(got.reshape(dates, plan.window, cols), region)

    own = plan.own_rows
    core, pair = me % 2, (me // 2) % 2
    other = swap(away, 2)
    gram = gram + swap(gram, 2)
    both = jnp.stack([jnp.where(pair == 0, stay, other), jnp.where(pair == 0, other, stay)], axis=1)
    low, high = both[:, :, :own], both[:, :, own:]
    mine = jnp.where(core == 0, low, high)
    theirs = swap(jnp.where(core == 0, high, low), 1)
    gram = gram + swap(gram, 1)
    smoothed = jnp.stack(
        [jnp.where(core == 0, mine, theirs), jnp.where(core == 0, theirs, mine)], axis=2
    ).reshape(dates, bands, own, cols)
    bit = bands * plan.shared
    while bit < devices:
        gram = gram + swap(gram, bit)
        bit *= 2
    similarity = lax.dynamic_slice_in_dim(gram, me * date_dev, date_dev, 0) / (bands * rows * cols)
    return smoothed, similarity


def solution(mesh):
    in_specs = (
        P(("groups", "dates"), None, None, None),
        P(("groups", "dates"), None, None),
        P("groups", None),
    )
    out_specs = (P("groups", None, "dates", None), P(("groups", "dates"), None))
    return jax.shard_map(local, mesh=mesh, in_specs=in_specs, out_specs=out_specs, check_vma=False)
```

```python
import functools

import jax
import jax.numpy as jnp
from jax import lax
from jax.experimental import pallas as pl
from jax.experimental.pallas import tpu as pltpu
from jax.sharding import PartitionSpec as P

REGIONS = 8
STEPS = 4
HALO = 8
SHARED = 2

CHUNK = 4
UNROLL = 7

lam_space = 0.2
lam_time = 0.08

LIMIT = 48 * 1024 * 1024


def phi(difference):
    return difference / (1.0 + difference * difference)


class Plan:
    def __init__(self, devices, bands, rows):
        self.devices, self.bands, self.rows = devices, bands, rows
        planes = devices // bands
        self.shared = min(SHARED, planes)
        self.slabs = planes // self.shared
        self.plane_rows = rows // planes
        self.own_rows = rows // devices
        self.slab_rows = rows // self.slabs
        margin = HALO * min(self.slabs - 1, 2)
        self.window = self.slab_rows + margin

    def slab(self, index):
        return index // (self.bands * self.shared)

    def start(self, index):
        first = self.slab(index) * self.slab_rows - HALO
        last = self.rows - self.window
        if isinstance(index, int):
            return min(max(first, 0), last)
        return jnp.clip(first, 0, last)


def anomaly_kernel(plan, scenes_ref, mask_ref, region_ref, send_ref, sums_ref):
    date_dev, bands, rows, cols = scenes_ref.shape
    tiles = rows // 8
    per_region = bands + 1

    def tile_rows(i):
        return pl.ds(pl.multiple_of(i * 8, 8), 8)

    for date in range(date_dev):

        def gather(i, sums):
            clear = mask_ref[date, tile_rows(i)] > 0
            label = jnp.where(clear, region_ref[tile_rows(i)], -1)
            values = [scenes_ref[date, band, tile_rows(i)].astype(jnp.float32) for band in range(bands)]
            out = []
            for g in range(REGIONS):
                here = label == g
                for band in range(bands):
                    out.append(sums[g * per_region + band] + jnp.where(here, values[band], 0.0))
                out.append(sums[g * per_region + bands] + jnp.where(here, 1.0, 0.0))
            return tuple(out)

        zero = jnp.zeros((8, cols), jnp.float32)
        sums = lax.fori_loop(0, tiles, gather, (zero,) * (REGIONS * per_region), unroll=min(tiles, 8))
        for i, total in enumerate(sums):
            sums_ref[date, i : i + 1] = jnp.sum(total, axis=0, keepdims=True)

    means = []
    for date in range(date_dev):
        totals = jnp.sum(sums_ref[date], axis=1, keepdims=True)
        for band in range(bands):
            means.append(
                [
                    totals[g * per_region + band : g * per_region + band + 1]
                    / (totals[g * per_region + bands : g * per_region + bands + 1] + 1.0)
                    for g in range(REGIONS)
                ]
            )

    region = region_ref[...]
    for date in range(date_dev):
        clear = mask_ref[date].astype(jnp.float32)
        for band in range(bands):
            mean = jnp.zeros((rows, cols), jnp.float32)
            for g in range(REGIONS):
                mean = jnp.where(region == g, jnp.broadcast_to(means[date * bands + band][g], (rows, cols)), mean)
            anomaly = (clear * (scenes_ref[date, band].astype(jnp.float32) - mean)).astype(jnp.bfloat16)
            for target in range(band, plan.devices, bands):
                first = plan.start(target)
                send_ref[target, date] = anomaly[first : first + plan.window]


def diffuse_kernel(plan, dates, got_ref, region_ref, stay_ref, send_ref, gram_ref, field_ref):
    window, cols = plan.window, got_ref.shape[-1]
    me = lax.axis_index("dates")
    start = plan.start(me)
    land = (region_ref[pl.ds(pl.multiple_of(start, 8), window)] > 0).astype(jnp.float32)
    row = lax.broadcasted_iota(jnp.int32, (window, cols), 0)
    col = lax.broadcasted_iota(jnp.int32, (window, cols), 1)
    down = jnp.where(row < window - 1, pltpu.roll(land, window - 1, 0), 0.0)
    right = jnp.where(col < cols - 1, pltpu.roll(land, cols - 1, 1), 0.0)
    row_weight = jnp.concatenate([lam_space * land * down] * CHUNK, axis=0)
    col_weight = jnp.concatenate([lam_space * land * right] * CHUNK, axis=0)
    source = lax.broadcasted_iota(jnp.int32, (cols, cols), 0)
    target = lax.broadcasted_iota(jnp.int32, (cols, cols), 1)
    same = (source == target).astype(jnp.float32)
    onward = ((source == target + 1).astype(jnp.float32) - same).astype(jnp.bfloat16)
    inflow = (same - (source + 1 == target).astype(jnp.float32)).astype(jnp.bfloat16)
    length, chunks = CHUNK * window, dates // CHUNK

    for step in range(STEPS):

        def read(t):
            ref = got_ref if step == 0 else field_ref
            return ref[pl.ds(pl.multiple_of(t * window, 8), length)].astype(jnp.float32)

        def advance(current, following, date_in):
            difference = jnp.dot(current.astype(jnp.bfloat16), onward, preferred_element_type=jnp.float32)
            col_flux = (col_weight * phi(difference)).astype(jnp.bfloat16)
            row_flux = row_weight * phi(pltpu.roll(current, length - 1, 0) - current)
            date_flux = lam_time * phi(following - current)
            new = (
                current
                + (row_flux - pltpu.roll(row_flux, 1, 0))
                + jnp.dot(col_flux, inflow, preferred_element_type=jnp.float32)
                + (date_flux - jnp.concatenate([date_in, date_flux[:-window]], axis=0))
            )
            return new, date_flux[-window:]

        def one(k, date_in):
            new, date_out = advance(read(k * CHUNK), read(k * CHUNK + 1), date_in)
            field_ref[pl.ds(pl.multiple_of(k * length, 8), length)] = new
            return date_out

        date_in = lax.fori_loop(
            0, chunks - 1, one, jnp.zeros((window, cols), jnp.float32), unroll=min(chunks - 1, UNROLL)
        )
        current = read((chunks - 1) * CHUNK)
        new, _ = advance(current, jnp.concatenate([current[window:], current[-window:]], axis=0), date_in)
        field_ref[pl.ds((chunks - 1) * length, length)] = new

    half = plan.plane_rows // 2
    pair = (me // 2) % 2
    plane_first = (me // plan.bands) * plan.plane_rows - start
    stay_first = pl.multiple_of(plane_first + pair * half, 8)
    send_first = pl.multiple_of(plane_first + (1 - pair) * half, 8)
    for t in range(dates):
        stay_ref[t] = field_ref[pl.ds(t * window + stay_first, half)].astype(jnp.bfloat16)
        send_ref[t] = field_ref[pl.ds(t * window + send_first, half)].astype(jnp.bfloat16)

    slab_first = plan.slab(me) * plan.slab_rows - start

    def gram(i, total):
        rows = jnp.concatenate(
            [field_ref[pl.ds(slab_first + 2 * i + j, dates, stride=window)] for j in range(2)], axis=1
        ).astype(jnp.bfloat16)
        return total + lax.dot_general(
            rows, rows, (((1,), (1,)), ((), ())), preferred_element_type=jnp.float32
        )

    gram_ref[...] = lax.fori_loop(
        0, plan.slab_rows // 2, gram, jnp.zeros((dates, dates), jnp.float32), unroll=min(8, plan.slab_rows // 2)
    )


def swap(x, bit):
    count = lax.axis_size("dates")
    return lax.ppermute(x, "dates", [(i, i ^ bit) for i in range(count)])


def local(scenes, cloud_mask, region):
    date_dev, bands, rows, cols = scenes.shape
    devices = lax.axis_size("dates")
    dates = date_dev * devices
    plan = Plan(devices, bands, rows)
    me = lax.axis_index("dates")
    vmem = pl.BlockSpec(memory_space=pltpu.VMEM)
    params = pltpu.CompilerParams(vmem_limit_bytes=LIMIT)

    send = pl.pallas_call(
        functools.partial(anomaly_kernel, plan),
        out_shape=jax.ShapeDtypeStruct((devices, date_dev, plan.window, cols), jnp.bfloat16),
        in_specs=[vmem] * 3,
        out_specs=vmem,
        scratch_shapes=[pltpu.VMEM((date_dev, REGIONS * (bands + 1), cols), jnp.float32)],
        compiler_params=params,
    )(scenes, cloud_mask, region)
    got = lax.all_to_all(send, "dates", split_axis=0, concat_axis=0, tiled=True)
    half = plan.plane_rows // 2
    stay, away, gram = pl.pallas_call(
        functools.partial(diffuse_kernel, plan, dates),
        out_shape=(
            jax.ShapeDtypeStruct((dates, half, cols), jnp.bfloat16),
            jax.ShapeDtypeStruct((dates, half, cols), jnp.bfloat16),
            jax.ShapeDtypeStruct((dates, dates), jnp.float32),
        ),
        in_specs=[vmem] * 2,
        out_specs=(vmem,) * 3,
        scratch_shapes=[pltpu.VMEM((dates * plan.window, cols), jnp.float32)],
        compiler_params=params,
    )(got.reshape(dates * plan.window, cols), region)

    own = plan.own_rows
    core, pair = me % 2, (me // 2) % 2
    other = swap(away, 2)
    gram = gram + swap(gram, 2)
    both = jnp.stack([jnp.where(pair == 0, stay, other), jnp.where(pair == 0, other, stay)], axis=1)
    low, high = both[:, :, :own], both[:, :, own:]
    mine = jnp.where(core == 0, low, high)
    theirs = swap(jnp.where(core == 0, high, low), 1)
    gram = gram + swap(gram, 1)
    smoothed = jnp.stack(
        [jnp.where(core == 0, mine, theirs), jnp.where(core == 0, theirs, mine)], axis=2
    ).reshape(dates, bands, own, cols)
    bit = bands * plan.shared
    while bit < devices:
        gram = gram + swap(gram, bit)
        bit *= 2
    similarity = lax.dynamic_slice_in_dim(gram, me * date_dev, date_dev, 0) / (bands * rows * cols)
    return smoothed, similarity


def solution(mesh):
    in_specs = (
        P(("groups", "dates"), None, None, None),
        P(("groups", "dates"), None, None),
        P("groups", None),
    )
    out_specs = (P("groups", None, "dates", None), P(("groups", "dates"), None))
    return jax.shard_map(local, mesh=mesh, in_specs=in_specs, out_specs=out_specs, check_vma=False)
```

```python
import functools

import jax
import jax.numpy as jnp
from jax import lax
from jax.experimental import pallas as pl
from jax.experimental.pallas import tpu as pltpu
from jax.sharding import PartitionSpec as P

REGIONS = 8
STEPS = 4
TILE = 8
SHARED = 2
CHUNK = 4
UNROLL = 7

lam_space = 0.2
lam_time = 0.08

LIMIT = 48 * 1024 * 1024


def phi(difference):
    return difference / (1.0 + difference * difference)


class Plan:
    def __init__(self, devices, date_dev, bands, rows):
        self.devices, self.date_dev, self.bands, self.rows = devices, date_dev, bands, rows
        self.dates = devices * date_dev
        planes = devices // bands
        self.shared = min(SHARED, planes)
        self.slabs = planes // self.shared
        self.plane_rows = rows // planes
        self.own_rows = rows // devices
        self.slab_rows = rows // self.slabs
        self.window = self.slab_rows + TILE * min(self.slabs - 1, 2)
        self.compact = self.slabs == 2 and date_dev == 2
        self.wire = 2 * self.slab_rows + TILE if self.compact else date_dev * self.window
        self.gram_blocks = max(1, 2 * self.dates // 128)
        self.gram_slots = self.gram_blocks * self.dates // self.own_rows

    def slab(self, index):
        return index // (self.bands * self.shared)

    def start(self, index):
        first = self.slab(index) * self.slab_rows - TILE
        last = self.rows - self.window
        if isinstance(index, int):
            return min(max(first, 0), last)
        return jnp.clip(first, 0, last)


def anomaly_kernel(plan, scenes_hbm, mask_hbm, region_hbm, send_ref, scenes_ref, mask_ref, region_ref, sums_ref, sems):
    date_dev, bands, rows, cols = scenes_ref.shape
    copies = [
        pltpu.make_async_copy(source, target, sems.at[i])
        for i, (source, target) in enumerate(
            ((scenes_hbm, scenes_ref), (mask_hbm, mask_ref), (region_hbm, region_ref))
        )
    ]
    for copy in copies:
        copy.start()
    for copy in copies:
        copy.wait()

    step = 2 * TILE
    tiles = rows // step
    per_region = bands + 1

    def tile_rows(i):
        return pl.ds(pl.multiple_of(i * step, step), step)

    for date in range(date_dev):

        def fold(x):
            return x[:TILE] + x[TILE:]

        def gather(i, sums):
            clear = mask_ref[date, tile_rows(i)] > 0
            label = jnp.where(clear, region_ref[tile_rows(i)], -1)
            values = [scenes_ref[date, band, tile_rows(i)].astype(jnp.float32) for band in range(bands)]
            out = []
            for g in range(REGIONS):
                here = label == g
                for band in range(bands):
                    out.append(sums[g * per_region + band] + fold(jnp.where(here, values[band], 0.0)))
                out.append(sums[g * per_region + bands] + fold(jnp.where(here, 1.0, 0.0)))
            return tuple(out)

        zero = jnp.zeros((TILE, cols), jnp.float32)
        sums = lax.fori_loop(0, tiles, gather, (zero,) * (REGIONS * per_region), unroll=min(tiles, 4))
        for i, total in enumerate(sums):
            sums_ref[date, i : i + 1] = jnp.sum(total, axis=0, keepdims=True)

    means = []
    for date in range(date_dev):
        totals = jnp.sum(sums_ref[date], axis=1, keepdims=True)
        for band in range(bands):
            means.append(
                [
                    totals[g * per_region + band : g * per_region + band + 1]
                    / (totals[g * per_region + bands : g * per_region + bands + 1] + 1.0)
                    for g in range(REGIONS)
                ]
            )

    region = region_ref[...]
    row = lax.broadcasted_iota(jnp.int32, (TILE, cols), 0)
    half = TILE // 2
    for band in range(bands):
        anomalies = []
        for date in range(date_dev):
            mean = jnp.zeros((rows, cols), jnp.float32)
            for g in range(REGIONS):
                mean = jnp.where(region == g, jnp.broadcast_to(means[date * bands + band][g], (rows, cols)), mean)
            clear = mask_ref[date].astype(jnp.float32)
            anomalies.append(clear * (scenes_ref[date, band].astype(jnp.float32) - mean))
        for target in range(band, plan.devices, bands):
            if plan.compact:
                slab, size = plan.slab(target), plan.slab_rows
                for date in range(date_dev):
                    send_ref[target, date * size : (date + 1) * size] = anomalies[date][
                        slab * size : (slab + 1) * size
                    ].astype(jnp.bfloat16)
                edge = size if slab == 0 else size - TILE
                wanted = row < half if slab == 0 else row >= half
                send_ref[target, 2 * size :] = jnp.where(
                    wanted,
                    anomalies[0][edge : edge + TILE],
                    pltpu.roll(anomalies[1][edge : edge + TILE], half, 0),
                ).astype(jnp.bfloat16)
            else:
                first, size = plan.start(target), plan.window
                for date in range(date_dev):
                    send_ref[target, date * size : (date + 1) * size] = anomalies[date][first : first + size].astype(
                        jnp.bfloat16
                    )


def store_gram(plan, slots_ref, first, gram):
    dates, own = plan.dates, plan.own_rows
    high = gram.astype(jnp.bfloat16).astype(jnp.float32)
    both = jnp.concatenate([high, gram - high], axis=1)
    width = min(2 * dates, 128)
    for block in range(plan.gram_blocks):
        part = both[:, block * width : (block + 1) * width].astype(jnp.bfloat16)
        for i in range(dates // own):
            slots_ref[first + block * (dates // own) + i, :, :width] = part[i * own : (i + 1) * own]


def load_gram(plan, slots_ref, first):
    dates, own = plan.dates, plan.own_rows
    width = min(2 * dates, 128)
    blocks = []
    for block in range(plan.gram_blocks):
        slots = [
            slots_ref[first + block * (dates // own) + i, :, :width].astype(jnp.float32)
            for i in range(dates // own)
        ]
        blocks.append(jnp.concatenate(slots, axis=0))
    both = blocks[0] if len(blocks) == 1 else jnp.concatenate(blocks, axis=1)
    return both[:, :dates] + both[:, dates:]


def diffuse_kernel(plan, got_ref, region_ref, message_ref, rest_ref, gram_ref, field_ref):
    window, dates, cols = plan.window, plan.dates, got_ref.shape[-1]
    me = lax.axis_index("dates")
    start = plan.start(me)
    slab_first = plan.slab(me) * plan.slab_rows - start
    land = (region_ref[pl.ds(pl.multiple_of(start, TILE), window)] > 0).astype(jnp.float32)
    row = lax.broadcasted_iota(jnp.int32, (window, cols), 0)
    col = lax.broadcasted_iota(jnp.int32, (window, cols), 1)
    down = jnp.where(row < window - 1, pltpu.roll(land, window - 1, 0), 0.0)
    right = jnp.where(col < cols - 1, pltpu.roll(land, cols - 1, 1), 0.0)
    row_weight = jnp.concatenate([lam_space * land * down] * CHUNK, axis=0)
    col_weight = jnp.concatenate([lam_space * land * right] * CHUNK, axis=0)
    source = lax.broadcasted_iota(jnp.int32, (cols, cols), 0)
    target = lax.broadcasted_iota(jnp.int32, (cols, cols), 1)
    same = (source == target).astype(jnp.float32)
    onward = ((source == target + 1).astype(jnp.float32) - same).astype(jnp.bfloat16)
    inflow = (same - (source + 1 == target).astype(jnp.float32)).astype(jnp.bfloat16)
    length, chunks = CHUNK * window, dates // CHUNK

    if plan.compact:
        size, half = plan.slab_rows, TILE // 2
        edge = jnp.where(slab_first == 0, size, 0)
        tile_row = lax.broadcasted_iota(jnp.int32, (TILE, cols), 0)
        wanted = (tile_row < half) == (slab_first == 0)
        for device in range(plan.devices):
            halos = got_ref[device, 2 * size :].astype(jnp.float32)
            for date, halo in enumerate((halos, pltpu.roll(halos, half, 0))):
                base = (2 * device + date) * window
                field_ref[pl.ds(pl.multiple_of(base + slab_first, TILE), size)] = got_ref[
                    device, date * size : (date + 1) * size
                ].astype(jnp.float32)
                field_ref[pl.ds(pl.multiple_of(base + edge, TILE), TILE)] = jnp.where(wanted, halo, 0.0)
    else:

        def unpack(device, carry):
            field_ref[pl.ds(pl.multiple_of(device * plan.wire, TILE), plan.wire)] = got_ref[device].astype(jnp.float32)
            return carry

        lax.fori_loop(0, plan.devices, unpack, 0)

    for step in range(STEPS):

        def read(t):
            return field_ref[pl.ds(pl.multiple_of(t * window, TILE), length)]

        def advance(current, following, date_in):
            difference = jnp.dot(current.astype(jnp.bfloat16), onward, preferred_element_type=jnp.float32)
            col_flux = (col_weight * phi(difference)).astype(jnp.bfloat16)
            row_flux = row_weight * phi(pltpu.roll(current, length - 1, 0) - current)
            date_flux = lam_time * phi(following - current)
            new = (
                current
                + (row_flux - pltpu.roll(row_flux, 1, 0))
                + jnp.dot(col_flux, inflow, preferred_element_type=jnp.float32)
                + (date_flux - jnp.concatenate([date_in, date_flux[:-window]], axis=0))
            )
            return new, date_flux[-window:]

        def one(k, date_in):
            new, date_out = advance(read(k * CHUNK), read(k * CHUNK + 1), date_in)
            field_ref[pl.ds(pl.multiple_of(k * length, TILE), length)] = new
            return date_out

        date_in = lax.fori_loop(
            0, chunks - 1, one, jnp.zeros((window, cols), jnp.float32), unroll=min(chunks - 1, UNROLL)
        )
        current = read((chunks - 1) * CHUNK)
        new, _ = advance(current, jnp.concatenate([current[window:], current[-window:]], axis=0), date_in)
        field_ref[pl.ds((chunks - 1) * length, length)] = new

    def gram_rows(i, total):
        rows = jnp.concatenate(
            [field_ref[pl.ds(slab_first + 2 * i + j, dates, stride=window)] for j in range(2)], axis=1
        ).astype(jnp.bfloat16)
        return total + lax.dot_general(
            rows, rows, (((1,), (1,)), ((), ())), preferred_element_type=jnp.float32
        )

    gram = lax.fori_loop(
        0, plan.slab_rows // 2, gram_rows, jnp.zeros((dates, dates), jnp.float32), unroll=min(8, plan.slab_rows // 2)
    )
    gram_ref[...] = gram
    store_gram(plan, message_ref, 2 * dates, gram)

    own = plan.own_rows
    place = me % plan.bands
    plane_first = (me // plan.bands) * plan.plane_rows - start

    def share(t, carry):
        for ref, slot, other in (
            (message_ref, t, 3), (message_ref, dates + t, 2), (rest_ref, t, 0), (rest_ref, dates + t, 1)
        ):
            first = plane_first + (place ^ other) * own
            ref[slot] = field_ref[pl.ds(t * window + first, own)].astype(jnp.bfloat16)
        return carry

    lax.fori_loop(0, dates, share, 0, unroll=8)


def relay_kernel(plan, got_ref, rest_ref, gram_ref, message_ref, total_ref):
    dates = plan.dates
    message_ref[:dates] = rest_ref[dates:]
    message_ref[dates : 2 * dates] = got_ref[dates : 2 * dates]
    total = gram_ref[...] + load_gram(plan, got_ref, 2 * dates)
    total_ref[...] = total
    store_gram(plan, message_ref, 2 * dates, total)


def total_kernel(plan, got_ref, gram_ref, total_ref):
    total_ref[...] = gram_ref[...] + load_gram(plan, got_ref, 2 * plan.dates)


def assemble_kernel(plan, rest_ref, first_ref, second_ref, out_ref):
    dates = plan.dates
    place = lax.axis_index("dates") % plan.bands
    out_ref[:, place] = rest_ref[:dates]
    out_ref[:, place ^ 3] = first_ref[:dates]
    out_ref[:, place ^ 1] = second_ref[:dates]
    out_ref[:, place ^ 2] = second_ref[dates : 2 * dates]


def swap(x, bits):
    count = lax.axis_size("dates")
    return lax.ppermute(x, "dates", [(i, i ^ bits) for i in range(count)])


def local(scenes, cloud_mask, region):
    date_dev, bands, rows, cols = scenes.shape
    devices = lax.axis_size("dates")
    plan = Plan(devices, date_dev, bands, rows)
    dates, own = plan.dates, plan.own_rows
    me = lax.axis_index("dates")
    vmem = pl.BlockSpec(memory_space=pltpu.VMEM)
    hbm = pl.BlockSpec(memory_space=pltpu.MemorySpace.HBM)
    params = pltpu.CompilerParams(vmem_limit_bytes=LIMIT)

    def shape(*sizes, dtype=jnp.bfloat16):
        return jax.ShapeDtypeStruct(sizes, dtype)

    send = pl.pallas_call(
        functools.partial(anomaly_kernel, plan),
        out_shape=shape(devices, plan.wire, cols),
        in_specs=[hbm] * 3,
        out_specs=vmem,
        scratch_shapes=[
            pltpu.VMEM(scenes.shape, scenes.dtype),
            pltpu.VMEM(cloud_mask.shape, cloud_mask.dtype),
            pltpu.VMEM(region.shape, region.dtype),
            pltpu.VMEM((date_dev, REGIONS * (bands + 1), cols), jnp.float32),
            pltpu.SemaphoreType.DMA((3,)),
        ],
        compiler_params=params,
    )(*(pltpu.with_memory_space_constraint(x, pltpu.MemorySpace.HBM) for x in (scenes, cloud_mask, region)))
    got = lax.all_to_all(send, "dates", split_axis=0, concat_axis=0, tiled=True)
    slots = 2 * dates + plan.gram_slots
    square = shape(dates, dates, dtype=jnp.float32)
    message, rest, gram = pl.pallas_call(
        functools.partial(diffuse_kernel, plan),
        out_shape=(shape(slots, own, cols), shape(2 * dates, own, cols), square),
        in_specs=[vmem] * 2,
        out_specs=(vmem,) * 3,
        scratch_shapes=[pltpu.VMEM((dates * plan.window, cols), jnp.float32)],
        compiler_params=params,
    )(got, region)
    first = swap(message, 3)
    message, gram = pl.pallas_call(
        functools.partial(relay_kernel, plan),
        out_shape=(shape(slots, own, cols), square),
        in_specs=[vmem] * 3,
        out_specs=(vmem,) * 2,
        compiler_params=params,
    )(first, rest, gram)
    second = swap(message, 1)
    gram = pl.pallas_call(
        functools.partial(total_kernel, plan),
        out_shape=square,
        in_specs=[vmem] * 2,
        out_specs=vmem,
        compiler_params=params,
    )(second, gram)

    bit = bands * plan.shared
    while 2 * bit < devices:
        gram = gram + swap(gram, bit + 1)
        bit *= 2

    def rows_of(index):
        return lax.dynamic_slice_in_dim(gram, index * date_dev, date_dev, 0)

    mine = rows_of(me)
    if bit < devices:
        mine = mine + swap(rows_of(me ^ (bit + 1)), bit + 1)
    smoothed = pl.pallas_call(
        functools.partial(assemble_kernel, plan),
        out_shape=shape(dates, bands, own, cols),
        in_specs=[vmem] * 3,
        out_specs=vmem,
        compiler_params=params,
        cost_estimate=pl.CostEstimate(flops=dates * bands * own * cols, bytes_accessed=dates * bands * own * cols * 4, transcendentals=0),
    )(rest, first, second)
    return smoothed, mine / (bands * rows * cols)


def solution(mesh):
    in_specs = (
        P(("groups", "dates"), None, None, None),
        P(("groups", "dates"), None, None),
        P("groups", None),
    )
    out_specs = (P("groups", None, "dates", None), P(("groups", "dates"), None))
    return jax.shard_map(local, mesh=mesh, in_specs=in_specs, out_specs=out_specs, check_vma=False)
```

```python
import functools

import jax
import jax.numpy as jnp
from jax import lax
from jax.experimental import pallas as pl
from jax.experimental.pallas import tpu as pltpu
from jax.sharding import PartitionSpec as P

REGIONS = 8
STEPS = 4
TILE = 8
SHARED = 2
CHUNK = 4
UNROLL = 7

lam_space = 0.2
lam_time = 0.08

LIMIT = 48 * 1024 * 1024
HEAVY = 10**10


def phi(difference):
    return difference / (1.0 + difference * difference)


class Plan:
    def __init__(self, devices, date_dev, bands, rows):
        self.devices, self.date_dev, self.bands, self.rows = devices, date_dev, bands, rows
        self.dates = devices * date_dev
        planes = devices // bands
        self.shared = min(SHARED, planes)
        self.slabs = planes // self.shared
        self.plane_rows = rows // planes
        self.own_rows = rows // devices
        self.slab_rows = rows // self.slabs
        self.window = self.slab_rows + TILE * min(self.slabs - 1, 2)
        self.compact = self.slabs == 2 and date_dev == 2
        self.wire = 2 * self.slab_rows + TILE if self.compact else date_dev * self.window

    def slab(self, index):
        return index // (self.bands * self.shared)

    def start(self, index):
        first = self.slab(index) * self.slab_rows - TILE
        last = self.rows - self.window
        if isinstance(index, int):
            return min(max(first, 0), last)
        return jnp.clip(first, 0, last)


def anomaly_kernel(plan, scenes_hbm, mask_hbm, region_hbm, send_ref, scenes_ref, mask_ref, region_ref, sums_ref, sems):
    date_dev, bands, rows, cols = scenes_ref.shape
    copies = [
        pltpu.make_async_copy(source, target, sems.at[i])
        for i, (source, target) in enumerate(
            ((scenes_hbm, scenes_ref), (mask_hbm, mask_ref), (region_hbm, region_ref))
        )
    ]
    for copy in copies:
        copy.start()
    for copy in copies:
        copy.wait()

    step = 2 * TILE
    tiles = rows // step
    per_region = bands + 1

    def tile_rows(i):
        return pl.ds(pl.multiple_of(i * step, step), step)

    for date in range(date_dev):

        def fold(x):
            return x[:TILE] + x[TILE:]

        def gather(i, sums):
            clear = mask_ref[date, tile_rows(i)] > 0
            label = jnp.where(clear, region_ref[tile_rows(i)], -1)
            values = [scenes_ref[date, band, tile_rows(i)].astype(jnp.float32) for band in range(bands)]
            out = []
            for g in range(REGIONS):
                here = label == g
                for band in range(bands):
                    out.append(sums[g * per_region + band] + fold(jnp.where(here, values[band], 0.0)))
                out.append(sums[g * per_region + bands] + fold(jnp.where(here, 1.0, 0.0)))
            return tuple(out)

        zero = jnp.zeros((TILE, cols), jnp.float32)
        sums = lax.fori_loop(0, tiles, gather, (zero,) * (REGIONS * per_region), unroll=min(tiles, 4))
        for i, total in enumerate(sums):
            sums_ref[date, i : i + 1] = jnp.sum(total, axis=0, keepdims=True)

    means = []
    for date in range(date_dev):
        totals = jnp.sum(sums_ref[date], axis=1, keepdims=True)
        for band in range(bands):
            means.append(
                [
                    totals[g * per_region + band : g * per_region + band + 1]
                    / (totals[g * per_region + bands : g * per_region + bands + 1] + 1.0)
                    for g in range(REGIONS)
                ]
            )

    region = region_ref[...]
    row = lax.broadcasted_iota(jnp.int32, (TILE, cols), 0)
    half = TILE // 2
    for band in range(bands):
        anomalies = []
        for date in range(date_dev):
            mean = jnp.zeros((rows, cols), jnp.float32)
            for g in range(REGIONS):
                mean = jnp.where(region == g, jnp.broadcast_to(means[date * bands + band][g], (rows, cols)), mean)
            clear = mask_ref[date].astype(jnp.float32)
            anomalies.append(clear * (scenes_ref[date, band].astype(jnp.float32) - mean))
        for target in range(band, plan.devices, bands):
            if plan.compact:
                slab, size = plan.slab(target), plan.slab_rows
                for date in range(date_dev):
                    send_ref[target, date * size : (date + 1) * size] = anomalies[date][
                        slab * size : (slab + 1) * size
                    ].astype(jnp.bfloat16)
                edge = size if slab == 0 else size - TILE
                wanted = row < half if slab == 0 else row >= half
                send_ref[target, 2 * size :] = jnp.where(
                    wanted,
                    anomalies[0][edge : edge + TILE],
                    pltpu.roll(anomalies[1][edge : edge + TILE], half, 0),
                ).astype(jnp.bfloat16)
            else:
                first, size = plan.start(target), plan.window
                for date in range(date_dev):
                    send_ref[target, date * size : (date + 1) * size] = anomalies[date][first : first + size].astype(
                        jnp.bfloat16
                    )


def diffuse_kernel(plan, got_ref, region_ref, gram_ref, field_ref):
    window, dates, cols = plan.window, plan.dates, got_ref.shape[-1]
    me = lax.axis_index("dates")
    start = plan.start(me)
    slab_first = plan.slab(me) * plan.slab_rows - start
    land = (region_ref[pl.ds(pl.multiple_of(start, TILE), window)] > 0).astype(jnp.float32)
    row = lax.broadcasted_iota(jnp.int32, (window, cols), 0)
    col = lax.broadcasted_iota(jnp.int32, (window, cols), 1)
    down = jnp.where(row < window - 1, pltpu.roll(land, window - 1, 0), 0.0)
    right = jnp.where(col < cols - 1, pltpu.roll(land, cols - 1, 1), 0.0)
    row_weight = jnp.concatenate([lam_space * land * down] * CHUNK, axis=0)
    col_weight = jnp.concatenate([lam_space * land * right] * CHUNK, axis=0)
    source = lax.broadcasted_iota(jnp.int32, (cols, cols), 0)
    target = lax.broadcasted_iota(jnp.int32, (cols, cols), 1)
    same = (source == target).astype(jnp.float32)
    onward = ((source == target + 1).astype(jnp.float32) - same).astype(jnp.bfloat16)
    inflow = (same - (source + 1 == target).astype(jnp.float32)).astype(jnp.bfloat16)
    length, chunks = CHUNK * window, dates // CHUNK

    if plan.compact:
        size, half = plan.slab_rows, TILE // 2
        edge = jnp.where(slab_first == 0, size, 0)
        tile_row = lax.broadcasted_iota(jnp.int32, (TILE, cols), 0)
        wanted = (tile_row < half) == (slab_first == 0)
        for device in range(plan.devices):
            halos = got_ref[device, 2 * size :].astype(jnp.float32)
            for date, halo in enumerate((halos, pltpu.roll(halos, half, 0))):
                base = (2 * device + date) * window
                field_ref[pl.ds(pl.multiple_of(base + slab_first, TILE), size)] = got_ref[
                    device, date * size : (date + 1) * size
                ].astype(jnp.float32)
                field_ref[pl.ds(pl.multiple_of(base + edge, TILE), TILE)] = jnp.where(wanted, halo, 0.0)
    else:

        def unpack(device, carry):
            field_ref[pl.ds(pl.multiple_of(device * plan.wire, TILE), plan.wire)] = got_ref[device].astype(jnp.float32)
            return carry

        lax.fori_loop(0, plan.devices, unpack, 0)

    for step in range(STEPS):

        def read(t):
            return field_ref[pl.ds(pl.multiple_of(t * window, TILE), length)]

        def advance(current, following, date_in):
            difference = jnp.dot(current.astype(jnp.bfloat16), onward, preferred_element_type=jnp.float32)
            col_flux = (col_weight * phi(difference)).astype(jnp.bfloat16)
            row_flux = row_weight * phi(pltpu.roll(current, length - 1, 0) - current)
            date_flux = lam_time * phi(following - current)
            new = (
                current
                + (row_flux - pltpu.roll(row_flux, 1, 0))
                + jnp.dot(col_flux, inflow, preferred_element_type=jnp.float32)
                + (date_flux - jnp.concatenate([date_in, date_flux[:-window]], axis=0))
            )
            return new, date_flux[-window:]

        def one(k, date_in):
            new, date_out = advance(read(k * CHUNK), read(k * CHUNK + 1), date_in)
            field_ref[pl.ds(pl.multiple_of(k * length, TILE), length)] = new
            return date_out

        date_in = lax.fori_loop(
            0, chunks - 1, one, jnp.zeros((window, cols), jnp.float32), unroll=min(chunks - 1, UNROLL)
        )
        current = read((chunks - 1) * CHUNK)
        new, _ = advance(current, jnp.concatenate([current[window:], current[-window:]], axis=0), date_in)
        field_ref[pl.ds((chunks - 1) * length, length)] = new

    def gram_rows(i, total):
        rows = jnp.concatenate(
            [field_ref[pl.ds(slab_first + 2 * i + j, dates, stride=window)] for j in range(2)], axis=1
        ).astype(jnp.bfloat16)
        return total + lax.dot_general(
            rows, rows, (((1,), (1,)), ((), ())), preferred_element_type=jnp.float32
        )

    gram_ref[...] = lax.fori_loop(
        0, plan.slab_rows // 2, gram_rows, jnp.zeros((dates, dates), jnp.float32), unroll=min(8, plan.slab_rows // 2)
    )


def share_kernel(plan, field_ref, gram_ref, message_ref, rest_ref):
    window, dates, own = plan.window, plan.dates, plan.own_rows
    me = lax.axis_index("dates")
    place = me % plan.bands
    plane_first = (me // plan.bands) * plan.plane_rows - plan.start(me)

    def share(t, carry):
        for ref, slot, other in (
            (message_ref, t, 3), (message_ref, dates + t, 2), (rest_ref, t, 0), (rest_ref, dates + t, 1)
        ):
            first = plane_first + (place ^ other) * own
            ref[slot] = field_ref[pl.ds(t * window + first, own)].astype(jnp.bfloat16)
        return carry

    lax.fori_loop(0, dates, share, 0, unroll=8)


def relay_kernel(plan, got_ref, rest_ref, message_ref):
    dates = plan.dates
    message_ref[:dates] = rest_ref[dates:]
    message_ref[dates:] = got_ref[dates:]


def sum_kernel(scale, mine_ref, other_ref, sim_ref):
    sim_ref[...] = (mine_ref[...] + other_ref[...]) * scale


def finish_kernel(plan, rest_ref, first_ref, second_ref, sim_ref, out_hbm, sim_hbm, sems):
    dates = plan.dates
    place = lax.axis_index("dates") % plan.bands
    head, tail = pl.ds(0, dates), pl.ds(dates, dates)
    copies = [
        pltpu.make_async_copy(source.at[part], out_hbm.at[:, place ^ other], sems.at[i])
        for i, (source, part, other) in enumerate(
            ((rest_ref, head, 0), (first_ref, head, 3), (second_ref, head, 1), (second_ref, tail, 2))
        )
    ]
    for copy in copies:
        copy.start()
    copies.append(pltpu.make_async_copy(sim_ref, sim_hbm, sems.at[4]))
    copies[-1].start()
    for copy in copies:
        copy.wait()


def swap(x, bits):
    count = lax.axis_size("dates")
    return lax.ppermute(x, "dates", [(i, i ^ bits) for i in range(count)])


def local(scenes, cloud_mask, region):
    date_dev, bands, rows, cols = scenes.shape
    devices = lax.axis_size("dates")
    plan = Plan(devices, date_dev, bands, rows)
    dates, own = plan.dates, plan.own_rows
    me = lax.axis_index("dates")
    vmem = pl.BlockSpec(memory_space=pltpu.VMEM)
    hbm = pl.BlockSpec(memory_space=pltpu.MemorySpace.HBM)
    params = pltpu.CompilerParams(vmem_limit_bytes=LIMIT)
    moved = dates * bands * own * cols
    small = pl.CostEstimate(flops=moved, bytes_accessed=4 * moved, transcendentals=0)

    def shape(*sizes, dtype=jnp.bfloat16):
        return jax.ShapeDtypeStruct(sizes, dtype)

    send = pl.pallas_call(
        functools.partial(anomaly_kernel, plan),
        out_shape=shape(devices, plan.wire, cols),
        in_specs=[hbm] * 3,
        out_specs=vmem,
        scratch_shapes=[
            pltpu.VMEM(scenes.shape, scenes.dtype),
            pltpu.VMEM(cloud_mask.shape, cloud_mask.dtype),
            pltpu.VMEM(region.shape, region.dtype),
            pltpu.VMEM((date_dev, REGIONS * (bands + 1), cols), jnp.float32),
            pltpu.SemaphoreType.DMA((3,)),
        ],
        compiler_params=params,
    )(*(pltpu.with_memory_space_constraint(x, pltpu.MemorySpace.HBM) for x in (scenes, cloud_mask, region)))
    got = lax.all_to_all(send, "dates", split_axis=0, concat_axis=0, tiled=True)
    gram, field = pl.pallas_call(
        functools.partial(diffuse_kernel, plan),
        out_shape=(shape(dates, dates, dtype=jnp.float32), shape(dates * plan.window, cols, dtype=jnp.float32)),
        in_specs=[vmem] * 2,
        out_specs=(vmem,) * 2,
        compiler_params=params,
    )(got, region)
    gram = gram + swap(gram, 3)
    rows_shape = shape(2 * dates, own, cols)
    message, rest = pl.pallas_call(
        functools.partial(share_kernel, plan),
        out_shape=(rows_shape, rows_shape),
        in_specs=[vmem] * 2,
        out_specs=(vmem,) * 2,
        compiler_params=params,
        cost_estimate=small,
    )(field, gram)
    first = swap(message, 3)
    gram = gram + swap(gram, 1)

    bit = bands * plan.shared
    while 2 * bit < devices:
        gram = gram + swap(gram, bit + 1)
        bit *= 2

    def rows_of(index):
        return lax.dynamic_slice_in_dim(gram, index * date_dev, date_dev, 0)

    mine = rows_of(me)
    other = swap(rows_of(me ^ (bit + 1)), bit + 1) if bit < devices else jnp.zeros_like(mine)
    message = pl.pallas_call(
        functools.partial(relay_kernel, plan),
        out_shape=rows_shape,
        in_specs=[vmem] * 2,
        out_specs=vmem,
        compiler_params=params,
        cost_estimate=small,
    )(first, rest)
    second = swap(message, 1)
    similarity = pl.pallas_call(
        functools.partial(sum_kernel, 1.0 / (bands * rows * cols)),
        out_shape=shape(date_dev, dates, dtype=jnp.float32),
        in_specs=[vmem] * 2,
        out_specs=vmem,
        compiler_params=params,
        cost_estimate=pl.CostEstimate(flops=HEAVY, bytes_accessed=HEAVY // 100, transcendentals=0),
    )(mine, other)
    return pl.pallas_call(
        functools.partial(finish_kernel, plan),
        out_shape=(shape(dates, bands, own, cols), shape(date_dev, dates, dtype=jnp.float32)),
        in_specs=[vmem] * 4,
        out_specs=(hbm,) * 2,
        scratch_shapes=[pltpu.SemaphoreType.DMA((5,))],
        compiler_params=params,
        cost_estimate=small,
    )(rest, first, second, similarity)


def solution(mesh):
    in_specs = (
        P(("groups", "dates"), None, None, None),
        P(("groups", "dates"), None, None),
        P("groups", None),
    )
    out_specs = (P("groups", None, "dates", None), P(("groups", "dates"), None))
    return jax.shard_map(local, mesh=mesh, in_specs=in_specs, out_specs=out_specs, check_vma=False)
```

```python
import functools

import jax
import jax.numpy as jnp
from jax import lax
from jax.experimental import pallas as pl
from jax.experimental.pallas import tpu as pltpu
from jax.sharding import PartitionSpec as P

REGIONS = 8
STEPS = 4
TILE = 8
SHARED = 2
UNROLL = 8

lam_space = 0.2
lam_time = 0.08

LIMIT = 48 * 1024 * 1024
HEAVY = 10**10


def phi(difference):
    return difference / (1.0 + difference * difference)


class Plan:
    def __init__(self, devices, date_dev, bands, rows):
        self.devices, self.date_dev, self.bands, self.rows = devices, date_dev, bands, rows
        self.dates = devices * date_dev
        planes = devices // bands
        self.shared = min(SHARED, planes)
        self.slabs = planes // self.shared
        self.plane_rows = rows // planes
        self.own_rows = rows // devices
        self.slab_rows = rows // self.slabs
        self.window = self.slab_rows + STEPS * min(self.slabs - 1, 2)
        self.fine = self.dates // TILE
        self.compact = self.slabs == 2 and date_dev == 2
        self.wire = 2 * self.slab_rows + TILE if self.compact else date_dev * self.window

    def slab(self, index):
        return index // (self.bands * self.shared)

    def start(self, index):
        first = self.slab(index) * self.slab_rows - STEPS
        last = self.rows - self.window
        if isinstance(index, int):
            return min(max(first, 0), last)
        return jnp.clip(first, 0, last)


def anomaly_kernel(plan, scenes_hbm, mask_hbm, region_hbm, send_ref, scenes_ref, mask_ref, region_ref, sums_ref, sems):
    date_dev, bands, rows, cols = scenes_ref.shape
    copies = [
        pltpu.make_async_copy(source, target, sems.at[i])
        for i, (source, target) in enumerate(
            ((scenes_hbm, scenes_ref), (mask_hbm, mask_ref), (region_hbm, region_ref))
        )
    ]
    for copy in copies:
        copy.start()
    for copy in copies:
        copy.wait()

    step = 2 * TILE
    tiles = rows // step
    per_region = bands + 1

    def tile_rows(i):
        return pl.ds(pl.multiple_of(i * step, step), step)

    for date in range(date_dev):

        def fold(x):
            return x[:TILE] + x[TILE:]

        def gather(i, sums):
            clear = mask_ref[date, tile_rows(i)] > 0
            label = jnp.where(clear, region_ref[tile_rows(i)], -1)
            values = [scenes_ref[date, band, tile_rows(i)].astype(jnp.float32) for band in range(bands)]
            out = []
            for g in range(REGIONS):
                here = label == g
                for band in range(bands):
                    out.append(sums[g * per_region + band] + fold(jnp.where(here, values[band], 0.0)))
                out.append(sums[g * per_region + bands] + fold(jnp.where(here, 1.0, 0.0)))
            return tuple(out)

        zero = jnp.zeros((TILE, cols), jnp.float32)
        sums = lax.fori_loop(0, tiles, gather, (zero,) * (REGIONS * per_region), unroll=min(tiles, 4))
        for i, total in enumerate(sums):
            sums_ref[date, i : i + 1] = jnp.sum(total, axis=0, keepdims=True)

    means = []
    for date in range(date_dev):
        totals = jnp.sum(sums_ref[date], axis=1, keepdims=True)
        for band in range(bands):
            means.append(
                [
                    totals[g * per_region + band : g * per_region + band + 1]
                    / (totals[g * per_region + bands : g * per_region + bands + 1] + 1.0)
                    for g in range(REGIONS)
                ]
            )

    region = region_ref[...]
    row = lax.broadcasted_iota(jnp.int32, (TILE, cols), 0)
    half = TILE // 2
    for band in range(bands):
        anomalies = []
        for date in range(date_dev):
            mean = jnp.zeros((rows, cols), jnp.float32)
            for g in range(REGIONS):
                mean = jnp.where(region == g, jnp.broadcast_to(means[date * bands + band][g], (rows, cols)), mean)
            clear = mask_ref[date].astype(jnp.float32)
            anomalies.append(clear * (scenes_ref[date, band].astype(jnp.float32) - mean))
        per_slab = bands * plan.shared
        for slab in range(plan.slabs):
            if plan.compact:
                size = plan.slab_rows
                blocks = [anomaly[slab * size : (slab + 1) * size] for anomaly in anomalies]
                edge = size if slab == 0 else size - TILE
                wanted = row < half if slab == 0 else row >= half
                other = pltpu.roll(anomalies[1][edge : edge + TILE], half, 0)
                blocks.append(jnp.where(wanted, anomalies[0][edge : edge + TILE], other))
            else:
                first = plan.start(slab * per_slab)
                blocks = [anomaly[first : first + plan.window] for anomaly in anomalies]
            offset = 0
            for block in blocks:
                block = block.astype(jnp.bfloat16)
                for target in range(slab * per_slab + band, (slab + 1) * per_slab, bands):
                    send_ref[target, offset : offset + block.shape[0]] = block
                offset += block.shape[0]


def diffuse_kernel(plan, got_ref, region_ref, gram_ref, field_ref, other_ref, wide_ref, land_ref, row_ref, col_ref, turn_ref):
    window, dates, fine, wire = plan.window, plan.dates, plan.fine, plan.wire
    cols = got_ref.shape[-1]
    me = lax.axis_index("dates")
    start = plan.start(me)
    slab = plan.slab(me)
    own_first = slab * plan.slab_rows - start

    land_ref[: plan.rows] = (region_ref[...] > 0).astype(jnp.float32)
    here = land_ref[pl.ds(start, window)]
    row = lax.broadcasted_iota(jnp.int32, (window, cols), 0)
    col = lax.broadcasted_iota(jnp.int32, (window, cols), 1)
    above = jnp.where(row > 0, pltpu.roll(here, 1, 0), 0.0)
    right = jnp.where(col < cols - 1, pltpu.roll(here, cols - 1, 1), 0.0)
    row_weight = lam_space * here * above
    col_weight = lam_space * here * right
    for r in range(window):
        row_ref[r * TILE : (r + 1) * TILE] = jnp.broadcast_to(row_weight[r : r + 1], (TILE, cols))
        col_ref[r * TILE : (r + 1) * TILE] = jnp.broadcast_to(col_weight[r : r + 1], (TILE, cols))
    row_ref[window * TILE :] = jnp.zeros((TILE, cols), jnp.float32)
    for ref in (field_ref, other_ref):
        ref[window * dates :] = jnp.zeros((dates, cols), jnp.float32)
    sublane = lax.broadcasted_iota(jnp.int32, (TILE, cols), 0)
    last_weight = jnp.where(sublane < TILE - 1, lam_time, 0.0)
    source = lax.broadcasted_iota(jnp.int32, (cols, cols), 0)
    target = lax.broadcasted_iota(jnp.int32, (cols, cols), 1)
    same = (source == target).astype(jnp.float32)
    onward = ((source == target + 1).astype(jnp.float32) - same).astype(jnp.bfloat16)
    inflow = (same - (source + 1 == target).astype(jnp.float32)).astype(jnp.bfloat16)

    def widen(device, carry):
        wide_ref[pl.ds(pl.multiple_of(device * wire, TILE), wire)] = got_ref[device].astype(jnp.float32)
        return carry

    lax.fori_loop(0, plan.devices, widen, 0, unroll=min(plan.devices, 16))
    old_ref, new_ref = (field_ref, other_ref) if STEPS % 2 == 0 else (other_ref, field_ref)
    stride = fine // plan.date_dev * wire

    def place(r, first, f):
        from_row = f // plan.date_dev * wire + first
        old_ref[pl.ds(pl.multiple_of(r * dates + f * TILE, TILE), TILE)] = wide_ref[pl.ds(from_row, TILE, stride=stride)]

    for f in range(fine):
        date = f % plan.date_dev
        if plan.compact:
            halo = 2 * plan.slab_rows + STEPS * jnp.where(slab == 0, date, 1 - date)
            halo_row = jnp.where(slab == 0, plan.slab_rows, 0)
            for i in range(plan.slab_rows):
                place(own_first + i, date * plan.slab_rows + i, f)
            for i in range(STEPS):
                place(halo_row + i, halo + i, f)
        else:
            for i in range(window):
                place(i, date * window + i, f)

    chunk = max(1, 128 // dates)

    for step in range(STEPS):
        if plan.compact:
            base, count = jnp.where(slab == 0, 0, step + 1), window - step - 1
        else:
            base, count = 0, window

        def rows(r, n):
            return pl.ds(pl.multiple_of(r * dates, TILE), n * dates)

        def weights(ref, r, n):
            parts = []
            for i in range(n):
                parts += [ref[pl.ds(pl.multiple_of((r + i) * TILE, TILE), TILE)]] * fine
            return jnp.concatenate(parts, axis=0)

        def advance(r, n, row_in):
            current, following = old_ref[rows(r, n)], old_ref[rows(r + 1, n)]
            difference = jnp.dot(current.astype(jnp.bfloat16), onward, preferred_element_type=jnp.float32)
            col_flux = (weights(col_ref, r, n) * phi(difference)).astype(jnp.bfloat16)
            row_flux = weights(row_ref, r + 1, n) * phi(following - current)
            if n > 1:
                row_before = jnp.concatenate([row_in, row_flux[:-dates]], axis=0)
            else:
                row_before = row_in
            date_change = []
            for i in range(n):
                x = current[i * dates : (i + 1) * dates]
                later = jnp.concatenate([x[TILE:], pltpu.roll(x[:TILE], TILE - 1, 0)], axis=0)
                flux = phi(later - x)
                flux = jnp.concatenate([lam_time * flux[:-TILE], last_weight * flux[-TILE:]], axis=0)
                date_change.append(flux - jnp.concatenate([pltpu.roll(flux[-TILE:], 1, 0), flux[:-TILE]], axis=0))
            new_ref[rows(r, n)] = (
                current
                + (row_flux - row_before)
                + jnp.dot(col_flux, inflow, preferred_element_type=jnp.float32)
                + (date_change[0] if n == 1 else jnp.concatenate(date_change, axis=0))
            )
            return row_flux[-dates:]

        before = old_ref[rows(jnp.maximum(base - 1, 0), 1)]
        row_in = weights(row_ref, base, 1) * phi(old_ref[rows(base, 1)] - before)
        full = count // chunk
        row_in = lax.fori_loop(
            0, full, lambda k, carry: advance(base + k * chunk, chunk, carry), row_in, unroll=min(full, UNROLL)
        )
        if count % chunk:
            advance(base + full * chunk, count % chunk, row_in)
        old_ref, new_ref = new_ref, old_ref

    def gram_rows(i, total):
        pair = [
            field_ref[pl.ds(pl.multiple_of((own_first + 2 * i + j) * dates, TILE), dates)].astype(jnp.bfloat16)
            for j in range(2)
        ]
        both = jnp.concatenate(pair, axis=1)
        return total + lax.dot_general(both, both, (((1,), (1,)), ((), ())), preferred_element_type=jnp.float32)

    gram = lax.fori_loop(
        0, plan.slab_rows // 2, gram_rows, jnp.zeros((dates, dates), jnp.float32), unroll=min(8, plan.slab_rows // 2)
    )
    width = turn_ref.shape[1]
    for last in (False, True):
        for block in range(dates // width):
            part = gram[:, block * width : (block + 1) * width]
            for f in range(fine):
                turn_ref[pl.ds(block * dates + f, TILE, stride=fine)] = part[f * TILE : (f + 1) * TILE]
            if last:
                gram_ref[:, block * width : (block + 1) * width] = turn_ref[block * dates : (block + 1) * dates]
        if not last:
            gram = jnp.concatenate(
                [turn_ref[block * dates : (block + 1) * dates].T for block in range(dates // width)], axis=0
            )


def share_kernel(plan, field_ref, message_ref, rest_ref):
    dates, fine, own = plan.dates, plan.fine, plan.own_rows
    me = lax.axis_index("dates")
    place = me % plan.bands
    plane_first = (me // plan.bands) * plan.plane_rows - plan.start(me)

    def share(t, carry):
        from_row = t % fine * TILE + t // fine
        for ref, slot, other in (
            (message_ref, t, 3), (message_ref, dates + t, 2), (rest_ref, t, 0), (rest_ref, dates + t, 1)
        ):
            first = (plane_first + (place ^ other) * own) * dates
            ref[slot] = field_ref[pl.ds(first + from_row, own, stride=dates)].astype(jnp.bfloat16)
        return carry

    lax.fori_loop(0, dates, share, 0, unroll=8)


def relay_kernel(plan, got_ref, rest_ref, message_ref):
    dates = plan.dates
    message_ref[:dates] = rest_ref[dates:]
    message_ref[dates:] = got_ref[dates:]


def sum_kernel(scale, mine_ref, other_ref, sim_ref):
    sim_ref[...] = (mine_ref[...] + other_ref[...]) * scale


def finish_kernel(plan, rest_ref, first_ref, second_ref, sim_ref, out_hbm, sim_hbm, sems):
    dates = plan.dates
    place = lax.axis_index("dates") % plan.bands
    head, tail = pl.ds(0, dates), pl.ds(dates, dates)
    copies = [
        pltpu.make_async_copy(source.at[part], out_hbm.at[:, place ^ other], sems.at[i])
        for i, (source, part, other) in enumerate(
            ((rest_ref, head, 0), (first_ref, head, 3), (second_ref, head, 1), (second_ref, tail, 2))
        )
    ]
    for copy in copies:
        copy.start()
    copies.append(pltpu.make_async_copy(sim_ref, sim_hbm, sems.at[4]))
    copies[-1].start()
    for copy in copies:
        copy.wait()


def add_kernel(gram_ref, got_ref, message_ref, sum_ref):
    sum_ref[...] = gram_ref[...] + got_ref[...]


def swap(x, bits):
    count = lax.axis_size("dates")
    return lax.ppermute(x, "dates", [(i, i ^ bits) for i in range(count)])


def local(scenes, cloud_mask, region):
    date_dev, bands, rows, cols = scenes.shape
    devices = lax.axis_size("dates")
    plan = Plan(devices, date_dev, bands, rows)
    dates, own = plan.dates, plan.own_rows
    me = lax.axis_index("dates")
    vmem = pl.BlockSpec(memory_space=pltpu.VMEM)
    hbm = pl.BlockSpec(memory_space=pltpu.MemorySpace.HBM)
    params = pltpu.CompilerParams(vmem_limit_bytes=LIMIT)
    moved = dates * bands * own * cols
    small = pl.CostEstimate(flops=moved, bytes_accessed=4 * moved, transcendentals=0)

    def shape(*sizes, dtype=jnp.bfloat16):
        return jax.ShapeDtypeStruct(sizes, dtype)

    send = pl.pallas_call(
        functools.partial(anomaly_kernel, plan),
        out_shape=shape(devices, plan.wire, cols),
        in_specs=[hbm] * 3,
        out_specs=vmem,
        scratch_shapes=[
            pltpu.VMEM(scenes.shape, scenes.dtype),
            pltpu.VMEM(cloud_mask.shape, cloud_mask.dtype),
            pltpu.VMEM(region.shape, region.dtype),
            pltpu.VMEM((date_dev, REGIONS * (bands + 1), cols), jnp.float32),
            pltpu.SemaphoreType.DMA((3,)),
        ],
        compiler_params=params,
    )(*(pltpu.with_memory_space_constraint(x, pltpu.MemorySpace.HBM) for x in (scenes, cloud_mask, region)))
    got = lax.all_to_all(send, "dates", split_axis=0, concat_axis=0, tiled=True)
    gram, field = pl.pallas_call(
        functools.partial(diffuse_kernel, plan),
        out_shape=(shape(dates, dates, dtype=jnp.float32), shape(dates * (plan.window + 1), cols, dtype=jnp.float32)),
        in_specs=[vmem] * 2,
        out_specs=(vmem,) * 2,
        scratch_shapes=[
            pltpu.VMEM((dates * (plan.window + 1), cols), jnp.float32),
            pltpu.VMEM((devices * plan.wire, cols), jnp.float32),
            pltpu.VMEM((rows, cols), jnp.float32),
            pltpu.VMEM(((plan.window + 1) * TILE, cols), jnp.float32),
            pltpu.VMEM((plan.window * TILE, cols), jnp.float32),
            pltpu.VMEM((dates * max(1, dates // 128), min(dates, 128)), jnp.float32),
        ],
        compiler_params=params,
    )(got, region)
    first_gram = swap(gram, 3)
    rows_shape = shape(2 * dates, own, cols)
    message, rest = pl.pallas_call(
        functools.partial(share_kernel, plan),
        out_shape=(rows_shape, rows_shape),
        in_specs=[vmem],
        out_specs=(vmem,) * 2,
        compiler_params=params,
        cost_estimate=small,
    )(field)
    first = swap(message, 3)
    gram = pl.pallas_call(
        add_kernel,
        out_shape=shape(dates, dates, dtype=jnp.float32),
        in_specs=[vmem] * 3,
        out_specs=vmem,
        compiler_params=params,
    )(gram, first_gram, message)
    gram = gram + swap(gram, 1)

    bit = bands * plan.shared
    while 2 * bit < devices:
        gram = gram + swap(gram, bit + 1)
        bit *= 2

    def rows_of(index):
        return lax.dynamic_slice_in_dim(gram, index * date_dev, date_dev, 0)

    mine = rows_of(me)
    other = swap(rows_of(me ^ (bit + 1)), bit + 1) if bit < devices else jnp.zeros_like(mine)
    message = pl.pallas_call(
        functools.partial(relay_kernel, plan),
        out_shape=rows_shape,
        in_specs=[vmem] * 2,
        out_specs=vmem,
        compiler_params=params,
        cost_estimate=small,
    )(first, rest)
    second = swap(message, 1)
    similarity = pl.pallas_call(
        functools.partial(sum_kernel, 1.0 / (bands * rows * cols)),
        out_shape=shape(date_dev, dates, dtype=jnp.float32),
        in_specs=[vmem] * 2,
        out_specs=vmem,
        compiler_params=params,
        cost_estimate=pl.CostEstimate(flops=HEAVY, bytes_accessed=HEAVY // 100, transcendentals=0),
    )(mine, other)
    return pl.pallas_call(
        functools.partial(finish_kernel, plan),
        out_shape=(shape(dates, bands, own, cols), shape(date_dev, dates, dtype=jnp.float32)),
        in_specs=[vmem] * 4,
        out_specs=(hbm,) * 2,
        scratch_shapes=[pltpu.SemaphoreType.DMA((5,))],
        compiler_params=params,
        cost_estimate=small,
    )(rest, first, second, similarity)


def solution(mesh):
    in_specs = (
        P(("groups", "dates"), None, None, None),
        P(("groups", "dates"), None, None),
        P("groups", None),
    )
    out_specs = (P("groups", None, "dates", None), P(("groups", "dates"), None))
    return jax.shard_map(local, mesh=mesh, in_specs=in_specs, out_specs=out_specs, check_vma=False)
```

```python
import functools

import jax
import jax.numpy as jnp
from jax import lax
from jax.experimental import pallas as pl
from jax.experimental.pallas import tpu as pltpu
from jax.sharding import PartitionSpec as P

REGIONS = 8
STEPS = 4
TILE = 8
SHARED = 2
UNROLL = 8

lam_space = 0.2
lam_time = 0.08

LIMIT = 48 * 1024 * 1024
HEAVY = 10**10


def phi(difference):
    return difference / (1.0 + difference * difference)


class Plan:
    def __init__(self, devices, date_dev, bands, rows):
        self.devices, self.date_dev, self.bands, self.rows = devices, date_dev, bands, rows
        self.dates = devices * date_dev
        planes = devices // bands
        self.shared = min(SHARED, planes)
        self.slabs = planes // self.shared
        self.plane_rows = rows // planes
        self.own_rows = rows // devices
        self.slab_rows = rows // self.slabs
        self.window = self.slab_rows + STEPS * min(self.slabs - 1, 2)
        self.fine = self.dates // TILE
        self.compact = self.slabs == 2 and date_dev == 2
        self.wire = 2 * self.slab_rows + TILE if self.compact else date_dev * self.window

    def slab(self, index):
        return index // (self.bands * self.shared)

    def start(self, index):
        first = self.slab(index) * self.slab_rows - STEPS
        last = self.rows - self.window
        if isinstance(index, int):
            return min(max(first, 0), last)
        return jnp.clip(first, 0, last)


def anomaly_kernel(plan, scenes_hbm, mask_hbm, region_hbm, send_ref, scenes_ref, mask_ref, region_ref, sums_ref, sems):
    date_dev, bands, rows, cols = scenes_ref.shape
    copies = [
        pltpu.make_async_copy(source, target, sems.at[i])
        for i, (source, target) in enumerate(
            ((scenes_hbm, scenes_ref), (mask_hbm, mask_ref), (region_hbm, region_ref))
        )
    ]
    for copy in copies:
        copy.start()
    for copy in copies:
        copy.wait()

    step = 2 * TILE
    tiles = rows // step
    per_region = bands + 1

    def tile_rows(i):
        return pl.ds(pl.multiple_of(i * step, step), step)

    for date in range(date_dev):

        def fold(x):
            return x[:TILE] + x[TILE:]

        def gather(i, sums):
            clear = mask_ref[date, tile_rows(i)] > 0
            label = jnp.where(clear, region_ref[tile_rows(i)], -1)
            values = [scenes_ref[date, band, tile_rows(i)].astype(jnp.float32) for band in range(bands)]
            out = []
            here = [label == g for g in range(REGIONS)]
            for value in (*values, 1.0):
                out += [sums[len(out) + g] + fold(jnp.where(here[g], value, 0.0)) for g in range(REGIONS)]
            return tuple(out)

        zero = jnp.zeros((TILE, cols), jnp.float32)
        sums = lax.fori_loop(0, tiles, gather, (zero,) * (REGIONS * per_region), unroll=min(tiles, 4))
        for i, total in enumerate(sums):
            sums_ref[date, i : i + 1] = jnp.sum(total, axis=0, keepdims=True)

    means = []
    for date in range(date_dev):
        totals = jnp.sum(sums_ref[date], axis=1, keepdims=True)
        counts = totals[bands * REGIONS :] + 1.0
        for band in range(bands):
            mean = totals[band * REGIONS : (band + 1) * REGIONS] / counts
            means.append([mean[g : g + 1] for g in range(REGIONS)])

    region = region_ref[...]
    row = lax.broadcasted_iota(jnp.int32, (TILE, cols), 0)
    half = TILE // 2
    for band in range(bands):
        anomalies = []
        for date in range(date_dev):
            mean = jnp.zeros((rows, cols), jnp.float32)
            for g in range(REGIONS):
                mean = jnp.where(region == g, jnp.broadcast_to(means[date * bands + band][g], (rows, cols)), mean)
            clear = mask_ref[date].astype(jnp.float32)
            anomalies.append(clear * (scenes_ref[date, band].astype(jnp.float32) - mean))
        per_slab = bands * plan.shared
        for slab in range(plan.slabs):
            if plan.compact:
                size = plan.slab_rows
                blocks = [anomaly[slab * size : (slab + 1) * size] for anomaly in anomalies]
                edge = size if slab == 0 else size - TILE
                wanted = row < half if slab == 0 else row >= half
                other = pltpu.roll(anomalies[1][edge : edge + TILE], half, 0)
                blocks.append(jnp.where(wanted, anomalies[0][edge : edge + TILE], other))
            else:
                first = plan.start(slab * per_slab)
                blocks = [anomaly[first : first + plan.window] for anomaly in anomalies]
            offset = 0
            for block in blocks:
                block = block.astype(jnp.bfloat16)
                for target in range(slab * per_slab + band, (slab + 1) * per_slab, bands):
                    send_ref[target, offset : offset + block.shape[0]] = block
                offset += block.shape[0]


def diffuse_kernel(plan, got_ref, region_ref, gram_ref, field_ref, other_ref, wide_ref, land_ref, row_ref, col_ref, turn_ref):
    window, dates, fine, wire = plan.window, plan.dates, plan.fine, plan.wire
    cols = got_ref.shape[-1]
    me = lax.axis_index("dates")
    start = plan.start(me)
    slab = plan.slab(me)
    own_first = slab * plan.slab_rows - start

    land_ref[: plan.rows] = (region_ref[...] > 0).astype(jnp.float32)
    here = land_ref[pl.ds(start, window)]
    row = lax.broadcasted_iota(jnp.int32, (window, cols), 0)
    col = lax.broadcasted_iota(jnp.int32, (window, cols), 1)
    above = jnp.where(row > 0, pltpu.roll(here, 1, 0), 0.0)
    right = jnp.where(col < cols - 1, pltpu.roll(here, cols - 1, 1), 0.0)
    row_weight = lam_space * here * above
    col_weight = lam_space * here * right
    for r in range(window):
        row_ref[r * TILE : (r + 1) * TILE] = jnp.broadcast_to(row_weight[r : r + 1], (TILE, cols))
        col_ref[r * TILE : (r + 1) * TILE] = jnp.broadcast_to(col_weight[r : r + 1], (TILE, cols))
    row_ref[window * TILE :] = jnp.zeros((TILE, cols), jnp.float32)
    for ref in (field_ref, other_ref):
        ref[window * dates :] = jnp.zeros((dates, cols), jnp.float32)
    sublane = lax.broadcasted_iota(jnp.int32, (TILE, cols), 0)
    last_weight = jnp.where(sublane < TILE - 1, lam_time, 0.0)
    source = lax.broadcasted_iota(jnp.int32, (cols, cols), 0)
    target = lax.broadcasted_iota(jnp.int32, (cols, cols), 1)
    same = (source == target).astype(jnp.float32)
    onward = ((source == target + 1).astype(jnp.float32) - same).astype(jnp.bfloat16)
    inflow = (same - (source + 1 == target).astype(jnp.float32)).astype(jnp.bfloat16)

    def widen(device, carry):
        wide_ref[pl.ds(pl.multiple_of(device * wire, TILE), wire)] = got_ref[device].astype(jnp.float32)
        return carry

    lax.fori_loop(0, plan.devices, widen, 0, unroll=min(plan.devices, 16))
    old_ref, new_ref = (field_ref, other_ref) if STEPS % 2 == 0 else (other_ref, field_ref)
    stride = fine // plan.date_dev * wire

    def place(r, first, f):
        from_row = f // plan.date_dev * wire + first
        old_ref[pl.ds(pl.multiple_of(r * dates + f * TILE, TILE), TILE)] = wide_ref[pl.ds(from_row, TILE, stride=stride)]

    for f in range(fine):
        date = f % plan.date_dev
        if plan.compact:
            halo = 2 * plan.slab_rows + STEPS * jnp.where(slab == 0, date, 1 - date)
            halo_row = jnp.where(slab == 0, plan.slab_rows, 0)
            for i in range(plan.slab_rows):
                place(own_first + i, date * plan.slab_rows + i, f)
            for i in range(STEPS):
                place(halo_row + i, halo + i, f)
        else:
            for i in range(window):
                place(i, date * window + i, f)

    chunk = max(1, 128 // dates)

    for step in range(STEPS):
        if plan.compact:
            base, count = jnp.where(slab == 0, 0, step + 1), window - step - 1
        else:
            base, count = 0, window

        def rows(r, n):
            return pl.ds(pl.multiple_of(r * dates, TILE), n * dates)

        def weights(ref, r, n):
            parts = []
            for i in range(n):
                parts += [ref[pl.ds(pl.multiple_of((r + i) * TILE, TILE), TILE)]] * fine
            return jnp.concatenate(parts, axis=0)

        def advance(r, n, row_in):
            current, following = old_ref[rows(r, n)], old_ref[rows(r + 1, n)]
            difference = jnp.dot(current.astype(jnp.bfloat16), onward, preferred_element_type=jnp.float32)
            col_flux = (weights(col_ref, r, n) * phi(difference)).astype(jnp.bfloat16)
            row_flux = weights(row_ref, r + 1, n) * phi(following - current)
            if n > 1:
                row_before = jnp.concatenate([row_in, row_flux[:-dates]], axis=0)
            else:
                row_before = row_in
            date_change = []
            for i in range(n):
                x = current[i * dates : (i + 1) * dates]
                later = jnp.concatenate([x[TILE:], pltpu.roll(x[:TILE], TILE - 1, 0)], axis=0)
                flux = phi(later - x)
                flux = jnp.concatenate([lam_time * flux[:-TILE], last_weight * flux[-TILE:]], axis=0)
                date_change.append(flux - jnp.concatenate([pltpu.roll(flux[-TILE:], 1, 0), flux[:-TILE]], axis=0))
            new_ref[rows(r, n)] = (
                current
                + (row_flux - row_before)
                + jnp.dot(col_flux, inflow, preferred_element_type=jnp.float32)
                + (date_change[0] if n == 1 else jnp.concatenate(date_change, axis=0))
            )
            return row_flux[-dates:]

        before = old_ref[rows(jnp.maximum(base - 1, 0), 1)]
        row_in = weights(row_ref, base, 1) * phi(old_ref[rows(base, 1)] - before)
        full = count // chunk
        row_in = lax.fori_loop(
            0, full, lambda k, carry: advance(base + k * chunk, chunk, carry), row_in, unroll=min(full, UNROLL)
        )
        if count % chunk:
            advance(base + full * chunk, count % chunk, row_in)
        old_ref, new_ref = new_ref, old_ref

    def gram_rows(i, total):
        pair = [
            field_ref[pl.ds(pl.multiple_of((own_first + 2 * i + j) * dates, TILE), dates)].astype(jnp.bfloat16)
            for j in range(2)
        ]
        both = jnp.concatenate(pair, axis=1)
        return total + lax.dot_general(both, both, (((1,), (1,)), ((), ())), preferred_element_type=jnp.float32)

    gram = lax.fori_loop(
        0, plan.slab_rows // 2, gram_rows, jnp.zeros((dates, dates), jnp.float32), unroll=min(8, plan.slab_rows // 2)
    )
    width = turn_ref.shape[1]
    for last in (False, True):
        for block in range(dates // width):
            part = gram[:, block * width : (block + 1) * width]
            for f in range(fine):
                turn_ref[pl.ds(block * dates + f, TILE, stride=fine)] = part[f * TILE : (f + 1) * TILE]
            if last:
                gram_ref[:, block * width : (block + 1) * width] = turn_ref[block * dates : (block + 1) * dates]
        if not last:
            gram = jnp.concatenate(
                [turn_ref[block * dates : (block + 1) * dates].T for block in range(dates // width)], axis=0
            )


def share_kernel(plan, field_ref, message_ref, rest_ref):
    dates, fine, own = plan.dates, plan.fine, plan.own_rows
    me = lax.axis_index("dates")
    place = me % plan.bands
    plane_first = (me // plan.bands) * plan.plane_rows - plan.start(me)

    def share(t, carry):
        from_row = t % fine * TILE + t // fine
        for ref, slot, other in (
            (message_ref, t, 3), (message_ref, dates + t, 2), (rest_ref, t, 0), (rest_ref, dates + t, 1)
        ):
            first = (plane_first + (place ^ other) * own) * dates
            ref[slot] = field_ref[pl.ds(first + from_row, own, stride=dates)].astype(jnp.bfloat16)
        return carry

    lax.fori_loop(0, dates, share, 0, unroll=8)


def relay_kernel(plan, got_ref, rest_ref, message_ref):
    dates = plan.dates
    message_ref[:dates] = rest_ref[dates:]
    message_ref[dates:] = got_ref[dates:]


def sum_kernel(scale, mine_ref, other_ref, sim_ref):
    sim_ref[...] = (mine_ref[...] + other_ref[...]) * scale


def finish_kernel(plan, rest_ref, first_ref, second_ref, sim_ref, out_hbm, sim_hbm, sems):
    dates = plan.dates
    place = lax.axis_index("dates") % plan.bands
    head, tail = pl.ds(0, dates), pl.ds(dates, dates)
    copies = [
        pltpu.make_async_copy(source.at[part], out_hbm.at[:, place ^ other], sems.at[i])
        for i, (source, part, other) in enumerate(
            ((rest_ref, head, 0), (first_ref, head, 3), (second_ref, head, 1), (second_ref, tail, 2))
        )
    ]
    for copy in copies:
        copy.start()
    copies.append(pltpu.make_async_copy(sim_ref, sim_hbm, sems.at[4]))
    copies[-1].start()
    for copy in copies:
        copy.wait()


def add_kernel(gram_ref, got_ref, message_ref, sum_ref):
    sum_ref[...] = gram_ref[...] + got_ref[...]


def swap(x, bits):
    count = lax.axis_size("dates")
    return lax.ppermute(x, "dates", [(i, i ^ bits) for i in range(count)])


def local(scenes, cloud_mask, region):
    date_dev, bands, rows, cols = scenes.shape
    devices = lax.axis_size("dates")
    plan = Plan(devices, date_dev, bands, rows)
    dates, own = plan.dates, plan.own_rows
    me = lax.axis_index("dates")
    vmem = pl.BlockSpec(memory_space=pltpu.VMEM)
    hbm = pl.BlockSpec(memory_space=pltpu.MemorySpace.HBM)
    params = pltpu.CompilerParams(vmem_limit_bytes=LIMIT)
    moved = dates * bands * own * cols
    small = pl.CostEstimate(flops=moved, bytes_accessed=4 * moved, transcendentals=0)

    def shape(*sizes, dtype=jnp.bfloat16):
        return jax.ShapeDtypeStruct(sizes, dtype)

    send = pl.pallas_call(
        functools.partial(anomaly_kernel, plan),
        out_shape=shape(devices, plan.wire, cols),
        in_specs=[hbm] * 3,
        out_specs=vmem,
        scratch_shapes=[
            pltpu.VMEM(scenes.shape, scenes.dtype),
            pltpu.VMEM(cloud_mask.shape, cloud_mask.dtype),
            pltpu.VMEM(region.shape, region.dtype),
            pltpu.VMEM((date_dev, REGIONS * (bands + 1), cols), jnp.float32),
            pltpu.SemaphoreType.DMA((3,)),
        ],
        compiler_params=params,
    )(*(pltpu.with_memory_space_constraint(x, pltpu.MemorySpace.HBM) for x in (scenes, cloud_mask, region)))
    got = lax.all_to_all(send, "dates", split_axis=0, concat_axis=0, tiled=True)
    gram, field = pl.pallas_call(
        functools.partial(diffuse_kernel, plan),
        out_shape=(shape(dates, dates, dtype=jnp.float32), shape(dates * (plan.window + 1), cols, dtype=jnp.float32)),
        in_specs=[vmem] * 2,
        out_specs=(vmem,) * 2,
        scratch_shapes=[
            pltpu.VMEM((dates * (plan.window + 1), cols), jnp.float32),
            pltpu.VMEM((devices * plan.wire, cols), jnp.float32),
            pltpu.VMEM((rows, cols), jnp.float32),
            pltpu.VMEM(((plan.window + 1) * TILE, cols), jnp.float32),
            pltpu.VMEM((plan.window * TILE, cols), jnp.float32),
            pltpu.VMEM((dates * max(1, dates // 128), min(dates, 128)), jnp.float32),
        ],
        compiler_params=params,
    )(got, region)
    first_gram = swap(gram, 1)
    rows_shape = shape(2 * dates, own, cols)
    message, rest = pl.pallas_call(
        functools.partial(share_kernel, plan),
        out_shape=(rows_shape, rows_shape),
        in_specs=[vmem],
        out_specs=(vmem,) * 2,
        compiler_params=params,
        cost_estimate=small,
    )(field)
    first = swap(message, 3)
    gram = pl.pallas_call(
        add_kernel,
        out_shape=shape(dates, dates, dtype=jnp.float32),
        in_specs=[vmem] * 3,
        out_specs=vmem,
        compiler_params=params,
    )(gram, first_gram, message)
    gram = gram + swap(gram, 3)

    bit = bands * plan.shared
    while 2 * bit < devices:
        gram = gram + swap(gram, bit + 1)
        bit *= 2

    def rows_of(index):
        return lax.dynamic_slice_in_dim(gram, index * date_dev, date_dev, 0)

    mine = rows_of(me)
    other = swap(rows_of(me ^ (bit + 1)), bit + 1) if bit < devices else jnp.zeros_like(mine)
    message = pl.pallas_call(
        functools.partial(relay_kernel, plan),
        out_shape=rows_shape,
        in_specs=[vmem] * 2,
        out_specs=vmem,
        compiler_params=params,
        cost_estimate=small,
    )(first, rest)
    second = swap(message, 1)
    similarity = pl.pallas_call(
        functools.partial(sum_kernel, 1.0 / (bands * rows * cols)),
        out_shape=shape(date_dev, dates, dtype=jnp.float32),
        in_specs=[vmem] * 2,
        out_specs=vmem,
        compiler_params=params,
        cost_estimate=pl.CostEstimate(flops=HEAVY, bytes_accessed=HEAVY // 100, transcendentals=0),
    )(mine, other)
    return pl.pallas_call(
        functools.partial(finish_kernel, plan),
        out_shape=(shape(dates, bands, own, cols), shape(date_dev, dates, dtype=jnp.float32)),
        in_specs=[vmem] * 4,
        out_specs=(hbm,) * 2,
        scratch_shapes=[pltpu.SemaphoreType.DMA((5,))],
        compiler_params=params,
        cost_estimate=small,
    )(rest, first, second, similarity)


def solution(mesh):
    in_specs = (
        P(("groups", "dates"), None, None, None),
        P(("groups", "dates"), None, None),
        P("groups", None),
    )
    out_specs = (P("groups", None, "dates", None), P(("groups", "dates"), None))
    return jax.shard_map(local, mesh=mesh, in_specs=in_specs, out_specs=out_specs, check_vma=False)
```

```python
import functools

import jax
import jax.numpy as jnp
from jax import lax
from jax.experimental import pallas as pl
from jax.experimental.pallas import tpu as pltpu
from jax.sharding import PartitionSpec as P

REGIONS = 8
STEPS = 4
TILE = 8
SHARED = 2
UNROLL = 8
GRAM_ROWS = 4

lam_space = 0.2
lam_time = 0.08

LIMIT = 48 * 1024 * 1024
HEAVY = 10**10


def phi(difference):
    return difference / (1.0 + difference * difference)


class Plan:
    def __init__(self, devices, date_dev, bands, rows):
        self.devices, self.date_dev, self.bands, self.rows = devices, date_dev, bands, rows
        self.dates = devices * date_dev
        planes = devices // bands
        self.shared = min(SHARED, planes)
        self.slabs = planes // self.shared
        self.plane_rows = rows // planes
        self.own_rows = rows // devices
        self.slab_rows = rows // self.slabs
        self.window = self.slab_rows + STEPS * min(self.slabs - 1, 2)
        self.fine = self.dates // TILE
        self.compact = self.slabs == 2 and date_dev == 2
        self.wire = 2 * self.slab_rows + TILE if self.compact else date_dev * self.window

    def slab(self, index):
        return index // (self.bands * self.shared)

    def start(self, index):
        first = self.slab(index) * self.slab_rows - STEPS
        last = self.rows - self.window
        if isinstance(index, int):
            return min(max(first, 0), last)
        return jnp.clip(first, 0, last)


def anomaly_kernel(plan, scenes_hbm, mask_hbm, region_hbm, send_ref, scenes_ref, mask_ref, region_ref, sums_ref, sems):
    date_dev, bands, rows, cols = scenes_ref.shape
    copies = [
        pltpu.make_async_copy(source, target, sems.at[i])
        for i, (source, target) in enumerate(
            ((scenes_hbm, scenes_ref), (mask_hbm, mask_ref), (region_hbm, region_ref))
        )
    ]
    for copy in copies:
        copy.start()
    for copy in copies:
        copy.wait()

    step = 2 * TILE
    tiles = rows // step
    per_region = bands + 1

    def tile_rows(i):
        return pl.ds(pl.multiple_of(i * step, step), step)

    for date in range(date_dev):

        def fold(x):
            return x[:TILE] + x[TILE:]

        def gather(i, sums):
            clear = mask_ref[date, tile_rows(i)] > 0
            label = jnp.where(clear, region_ref[tile_rows(i)], -1)
            values = [scenes_ref[date, band, tile_rows(i)].astype(jnp.float32) for band in range(bands)]
            out = []
            here = [label == g for g in range(REGIONS)]
            for value in (*values, 1.0):
                out += [sums[len(out) + g] + fold(jnp.where(here[g], value, 0.0)) for g in range(REGIONS)]
            return tuple(out)

        zero = jnp.zeros((TILE, cols), jnp.float32)
        sums = lax.fori_loop(0, tiles, gather, (zero,) * (REGIONS * per_region), unroll=min(tiles, 4))
        for i, total in enumerate(sums):
            sums_ref[date, i : i + 1] = jnp.sum(total, axis=0, keepdims=True)

    means = []
    for date in range(date_dev):
        totals = jnp.sum(sums_ref[date], axis=1, keepdims=True)
        counts = totals[bands * REGIONS :] + 1.0
        for band in range(bands):
            mean = totals[band * REGIONS : (band + 1) * REGIONS] / counts
            means.append([mean[g : g + 1] for g in range(REGIONS)])

    region = region_ref[...]
    row = lax.broadcasted_iota(jnp.int32, (TILE, cols), 0)
    half = TILE // 2
    for band in range(bands):
        anomalies = []
        for date in range(date_dev):
            mean = jnp.zeros((rows, cols), jnp.float32)
            for g in range(REGIONS):
                mean = jnp.where(region == g, jnp.broadcast_to(means[date * bands + band][g], (rows, cols)), mean)
            clear = mask_ref[date].astype(jnp.float32)
            anomalies.append(clear * (scenes_ref[date, band].astype(jnp.float32) - mean))
        per_slab = bands * plan.shared
        for slab in range(plan.slabs):
            if plan.compact:
                size = plan.slab_rows
                blocks = [anomaly[slab * size : (slab + 1) * size] for anomaly in anomalies]
                edge = size if slab == 0 else size - TILE
                wanted = row < half if slab == 0 else row >= half
                other = pltpu.roll(anomalies[1][edge : edge + TILE], half, 0)
                blocks.append(jnp.where(wanted, anomalies[0][edge : edge + TILE], other))
            else:
                first = plan.start(slab * per_slab)
                blocks = [anomaly[first : first + plan.window] for anomaly in anomalies]
            offset = 0
            for block in blocks:
                block = block.astype(jnp.bfloat16)
                for target in range(slab * per_slab + band, (slab + 1) * per_slab, bands):
                    send_ref[target, offset : offset + block.shape[0]] = block
                offset += block.shape[0]


def diffuse_kernel(plan, got_ref, region_ref, gram_ref, field_ref, other_ref, wide_ref, land_ref, row_ref, col_ref, turn_ref):
    window, dates, fine, wire = plan.window, plan.dates, plan.fine, plan.wire
    cols = got_ref.shape[-1]
    me = lax.axis_index("dates")
    start = plan.start(me)
    slab = plan.slab(me)
    own_first = slab * plan.slab_rows - start

    land_ref[: plan.rows] = (region_ref[...] > 0).astype(jnp.float32)
    here = land_ref[pl.ds(start, window)]
    row = lax.broadcasted_iota(jnp.int32, (window, cols), 0)
    col = lax.broadcasted_iota(jnp.int32, (window, cols), 1)
    above = jnp.where(row > 0, pltpu.roll(here, 1, 0), 0.0)
    right = jnp.where(col < cols - 1, pltpu.roll(here, cols - 1, 1), 0.0)
    row_weight = lam_space * here * above
    col_weight = lam_space * here * right
    for r in range(window):
        row_ref[r * TILE : (r + 1) * TILE] = jnp.broadcast_to(row_weight[r : r + 1], (TILE, cols))
        col_ref[r * TILE : (r + 1) * TILE] = jnp.broadcast_to(col_weight[r : r + 1], (TILE, cols))
    row_ref[window * TILE :] = jnp.zeros((TILE, cols), jnp.float32)
    for ref in (field_ref, other_ref):
        ref[window * dates :] = jnp.zeros((dates, cols), jnp.float32)
    sublane = lax.broadcasted_iota(jnp.int32, (TILE, cols), 0)
    last_weight = jnp.where(sublane < TILE - 1, lam_time, 0.0)
    source = lax.broadcasted_iota(jnp.int32, (cols, cols), 0)
    target = lax.broadcasted_iota(jnp.int32, (cols, cols), 1)
    same = (source == target).astype(jnp.float32)
    onward = ((source == target + 1).astype(jnp.float32) - same).astype(jnp.bfloat16)
    inflow = (same - (source + 1 == target).astype(jnp.float32)).astype(jnp.bfloat16)

    def widen(device, carry):
        wide_ref[pl.ds(pl.multiple_of(device * wire, TILE), wire)] = got_ref[device].astype(jnp.float32)
        return carry

    lax.fori_loop(0, plan.devices, widen, 0, unroll=min(plan.devices, 16))
    old_ref, new_ref = (field_ref, other_ref) if STEPS % 2 == 0 else (other_ref, field_ref)
    stride = fine // plan.date_dev * wire

    def place(r, first, f):
        from_row = f // plan.date_dev * wire + first
        old_ref[pl.ds(pl.multiple_of(r * dates + f * TILE, TILE), TILE)] = wide_ref[pl.ds(from_row, TILE, stride=stride)]

    for f in range(fine):
        date = f % plan.date_dev
        if plan.compact:
            halo = 2 * plan.slab_rows + STEPS * jnp.where(slab == 0, date, 1 - date)
            halo_row = jnp.where(slab == 0, plan.slab_rows, 0)
            for i in range(plan.slab_rows):
                place(own_first + i, date * plan.slab_rows + i, f)
            for i in range(STEPS):
                place(halo_row + i, halo + i, f)
        else:
            for i in range(window):
                place(i, date * window + i, f)

    chunk = max(1, 256 // dates)

    for step in range(STEPS):
        if plan.compact:
            base, count = jnp.where(slab == 0, 0, step + 1), window - step - 1
        else:
            base, count = 0, window

        def rows(r, n):
            return pl.ds(pl.multiple_of(r * dates, TILE), n * dates)

        def weights(ref, r, n):
            parts = []
            for i in range(n):
                parts += [ref[pl.ds(pl.multiple_of((r + i) * TILE, TILE), TILE)]] * fine
            return jnp.concatenate(parts, axis=0)

        def advance(r, n, row_in):
            current, following = old_ref[rows(r, n)], old_ref[rows(r + 1, n)]
            difference = jnp.dot(current.astype(jnp.bfloat16), onward, preferred_element_type=jnp.float32)
            col_flux = (weights(col_ref, r, n) * phi(difference)).astype(jnp.bfloat16)
            row_flux = weights(row_ref, r + 1, n) * phi(following - current)
            if n > 1:
                row_before = jnp.concatenate([row_in, row_flux[:-dates]], axis=0)
            else:
                row_before = row_in
            date_change = []
            for i in range(n):
                x = current[i * dates : (i + 1) * dates]
                later = jnp.concatenate([x[TILE:], pltpu.roll(x[:TILE], TILE - 1, 0)], axis=0)
                flux = phi(later - x)
                flux = jnp.concatenate([lam_time * flux[:-TILE], last_weight * flux[-TILE:]], axis=0)
                date_change.append(flux - jnp.concatenate([pltpu.roll(flux[-TILE:], 1, 0), flux[:-TILE]], axis=0))
            new_ref[rows(r, n)] = (
                current
                + (row_flux - row_before)
                + jnp.dot(col_flux, inflow, preferred_element_type=jnp.float32)
                + (date_change[0] if n == 1 else jnp.concatenate(date_change, axis=0))
            )
            return row_flux[-dates:]

        before = old_ref[rows(jnp.maximum(base - 1, 0), 1)]
        row_in = weights(row_ref, base, 1) * phi(old_ref[rows(base, 1)] - before)
        full = count // chunk
        row_in = lax.fori_loop(
            0, full, lambda k, carry: advance(base + k * chunk, chunk, carry), row_in, unroll=min(full, UNROLL)
        )
        if count % chunk:
            advance(base + full * chunk, count % chunk, row_in)
        old_ref, new_ref = new_ref, old_ref

    def gram_rows(i, total):
        pair = [
            field_ref[pl.ds(pl.multiple_of((own_first + GRAM_ROWS * i + j) * dates, TILE), dates)].astype(jnp.bfloat16)
            for j in range(GRAM_ROWS)
        ]
        both = jnp.concatenate(pair, axis=1)
        return total + lax.dot_general(both, both, (((1,), (1,)), ((), ())), preferred_element_type=jnp.float32)

    gram = lax.fori_loop(
        0, plan.slab_rows // GRAM_ROWS, gram_rows, jnp.zeros((dates, dates), jnp.float32), unroll=min(8, plan.slab_rows // GRAM_ROWS)
    )
    width = turn_ref.shape[1]
    for last in (False, True):
        for block in range(dates // width):
            part = gram[:, block * width : (block + 1) * width]
            for f in range(fine):
                turn_ref[pl.ds(block * dates + f, TILE, stride=fine)] = part[f * TILE : (f + 1) * TILE]
            if last:
                gram_ref[:, block * width : (block + 1) * width] = turn_ref[block * dates : (block + 1) * dates]
        if not last:
            gram = jnp.concatenate(
                [turn_ref[block * dates : (block + 1) * dates].T for block in range(dates // width)], axis=0
            )


def share_kernel(plan, field_ref, message_ref, rest_ref):
    dates, fine, own = plan.dates, plan.fine, plan.own_rows
    me = lax.axis_index("dates")
    place = me % plan.bands
    plane_first = (me // plan.bands) * plan.plane_rows - plan.start(me)

    def share(t, carry):
        from_row = t % fine * TILE + t // fine
        for ref, slot, other in (
            (message_ref, t, 3), (message_ref, dates + t, 2), (rest_ref, t, 0), (rest_ref, dates + t, 1)
        ):
            first = (plane_first + (place ^ other) * own) * dates
            ref[slot] = field_ref[pl.ds(first + from_row, own, stride=dates)].astype(jnp.bfloat16)
        return carry

    lax.fori_loop(0, dates, share, 0, unroll=8)


def relay_kernel(plan, got_ref, rest_ref, message_ref):
    dates = plan.dates
    message_ref[:dates] = rest_ref[dates:]
    message_ref[dates:] = got_ref[dates:]


def sum_kernel(scale, mine_ref, other_ref, sim_ref):
    sim_ref[...] = (mine_ref[...] + other_ref[...]) * scale


def finish_kernel(plan, rest_ref, first_ref, second_ref, sim_ref, out_hbm, sim_hbm, sems):
    dates = plan.dates
    place = lax.axis_index("dates") % plan.bands
    head, tail = pl.ds(0, dates), pl.ds(dates, dates)
    copies = [
        pltpu.make_async_copy(source.at[part], out_hbm.at[:, place ^ other], sems.at[i])
        for i, (source, part, other) in enumerate(
            ((rest_ref, head, 0), (first_ref, head, 3), (second_ref, head, 1), (second_ref, tail, 2))
        )
    ]
    for copy in copies:
        copy.start()
    copies.append(pltpu.make_async_copy(sim_ref, sim_hbm, sems.at[4]))
    copies[-1].start()
    for copy in copies:
        copy.wait()


def add_kernel(gram_ref, got_ref, message_ref, sum_ref):
    sum_ref[...] = gram_ref[...] + got_ref[...]


def swap(x, bits):
    count = lax.axis_size("dates")
    return lax.ppermute(x, "dates", [(i, i ^ bits) for i in range(count)])


def local(scenes, cloud_mask, region):
    date_dev, bands, rows, cols = scenes.shape
    devices = lax.axis_size("dates")
    plan = Plan(devices, date_dev, bands, rows)
    dates, own = plan.dates, plan.own_rows
    me = lax.axis_index("dates")
    vmem = pl.BlockSpec(memory_space=pltpu.VMEM)
    hbm = pl.BlockSpec(memory_space=pltpu.MemorySpace.HBM)
    params = pltpu.CompilerParams(vmem_limit_bytes=LIMIT)
    moved = dates * bands * own * cols
    small = pl.CostEstimate(flops=moved, bytes_accessed=4 * moved, transcendentals=0)

    def shape(*sizes, dtype=jnp.bfloat16):
        return jax.ShapeDtypeStruct(sizes, dtype)

    send = pl.pallas_call(
        functools.partial(anomaly_kernel, plan),
        out_shape=shape(devices, plan.wire, cols),
        in_specs=[hbm] * 3,
        out_specs=vmem,
        scratch_shapes=[
            pltpu.VMEM(scenes.shape, scenes.dtype),
            pltpu.VMEM(cloud_mask.shape, cloud_mask.dtype),
            pltpu.VMEM(region.shape, region.dtype),
            pltpu.VMEM((date_dev, REGIONS * (bands + 1), cols), jnp.float32),
            pltpu.SemaphoreType.DMA((3,)),
        ],
        compiler_params=params,
    )(*(pltpu.with_memory_space_constraint(x, pltpu.MemorySpace.HBM) for x in (scenes, cloud_mask, region)))
    got = lax.all_to_all(send, "dates", split_axis=0, concat_axis=0, tiled=True)
    gram, field = pl.pallas_call(
        functools.partial(diffuse_kernel, plan),
        out_shape=(shape(dates, dates, dtype=jnp.float32), shape(dates * (plan.window + 1), cols, dtype=jnp.float32)),
        in_specs=[vmem] * 2,
        out_specs=(vmem,) * 2,
        scratch_shapes=[
            pltpu.VMEM((dates * (plan.window + 1), cols), jnp.float32),
            pltpu.VMEM((devices * plan.wire, cols), jnp.float32),
            pltpu.VMEM((rows, cols), jnp.float32),
            pltpu.VMEM(((plan.window + 1) * TILE, cols), jnp.float32),
            pltpu.VMEM((plan.window * TILE, cols), jnp.float32),
            pltpu.VMEM((dates * max(1, dates // 128), min(dates, 128)), jnp.float32),
        ],
        compiler_params=params,
    )(got, region)
    first_gram = swap(gram, 1)
    rows_shape = shape(2 * dates, own, cols)
    message, rest = pl.pallas_call(
        functools.partial(share_kernel, plan),
        out_shape=(rows_shape, rows_shape),
        in_specs=[vmem],
        out_specs=(vmem,) * 2,
        compiler_params=params,
        cost_estimate=small,
    )(field)
    first = swap(message, 3)
    gram = pl.pallas_call(
        add_kernel,
        out_shape=shape(dates, dates, dtype=jnp.float32),
        in_specs=[vmem] * 3,
        out_specs=vmem,
        compiler_params=params,
    )(gram, first_gram, message)
    gram = gram + swap(gram, 3)

    bit = bands * plan.shared
    while 2 * bit < devices:
        gram = gram + swap(gram, bit + 1)
        bit *= 2

    def rows_of(index):
        return lax.dynamic_slice_in_dim(gram, index * date_dev, date_dev, 0)

    mine = rows_of(me)
    other = swap(rows_of(me ^ (bit + 1)), bit + 1) if bit < devices else jnp.zeros_like(mine)
    message = pl.pallas_call(
        functools.partial(relay_kernel, plan),
        out_shape=rows_shape,
        in_specs=[vmem] * 2,
        out_specs=vmem,
        compiler_params=params,
        cost_estimate=small,
    )(first, rest)
    second = swap(message, 1)
    similarity = pl.pallas_call(
        functools.partial(sum_kernel, 1.0 / (bands * rows * cols)),
        out_shape=shape(date_dev, dates, dtype=jnp.float32),
        in_specs=[vmem] * 2,
        out_specs=vmem,
        compiler_params=params,
        cost_estimate=pl.CostEstimate(flops=HEAVY, bytes_accessed=HEAVY // 100, transcendentals=0),
    )(mine, other)
    return pl.pallas_call(
        functools.partial(finish_kernel, plan),
        out_shape=(shape(dates, bands, own, cols), shape(date_dev, dates, dtype=jnp.float32)),
        in_specs=[vmem] * 4,
        out_specs=(hbm,) * 2,
        scratch_shapes=[pltpu.SemaphoreType.DMA((5,))],
        compiler_params=params,
        cost_estimate=small,
    )(rest, first, second, similarity)


def solution(mesh):
    in_specs = (
        P(("groups", "dates"), None, None, None),
        P(("groups", "dates"), None, None),
        P("groups", None),
    )
    out_specs = (P("groups", None, "dates", None), P(("groups", "dates"), None))
    return jax.shard_map(local, mesh=mesh, in_specs=in_specs, out_specs=out_specs, check_vma=False)
```

```python
import functools

import jax
import jax.numpy as jnp
from jax import lax
from jax.experimental import pallas as pl
from jax.experimental.pallas import tpu as pltpu
from jax.sharding import PartitionSpec as P

REGIONS = 8
STEPS = 4
TILE = 8
SHARED = 2
UNROLL = 8

lam_space = 0.2
lam_time = 0.08

LIMIT = 48 * 1024 * 1024
HEAVY = 10**10


def phi(difference):
    return difference / (1.0 + difference * difference)


class Plan:
    def __init__(self, devices, date_dev, bands, rows):
        self.devices, self.date_dev, self.bands, self.rows = devices, date_dev, bands, rows
        self.dates = devices * date_dev
        planes = devices // bands
        self.shared = min(SHARED, planes)
        self.slabs = planes // self.shared
        self.plane_rows = rows // planes
        self.own_rows = rows // devices
        self.slab_rows = rows // self.slabs
        self.window = self.slab_rows + STEPS * min(self.slabs - 1, 2)
        self.fine = self.dates // TILE
        self.compact = self.slabs == 2 and date_dev == 2
        self.wire = 2 * self.slab_rows + TILE if self.compact else date_dev * self.window

    def slab(self, index):
        return index // (self.bands * self.shared)

    def start(self, index):
        first = self.slab(index) * self.slab_rows - STEPS
        last = self.rows - self.window
        if isinstance(index, int):
            return min(max(first, 0), last)
        return jnp.clip(first, 0, last)


def anomaly_kernel(plan, scenes_hbm, mask_hbm, region_hbm, send_ref, scenes_ref, mask_ref, region_ref, sums_ref, sems):
    date_dev, bands, rows, cols = scenes_ref.shape
    copies = [
        pltpu.make_async_copy(source, target, sems.at[i])
        for i, (source, target) in enumerate(
            ((scenes_hbm, scenes_ref), (mask_hbm, mask_ref), (region_hbm, region_ref))
        )
    ]
    for copy in copies:
        copy.start()
    for copy in copies:
        copy.wait()

    step = 2 * TILE
    tiles = rows // step
    per_region = bands + 1

    def tile_rows(i):
        return pl.ds(pl.multiple_of(i * step, step), step)

    for date in range(date_dev):

        def fold(x):
            return x[:TILE] + x[TILE:]

        def gather(i, sums):
            clear = mask_ref[date, tile_rows(i)] > 0
            label = jnp.where(clear, region_ref[tile_rows(i)], -1)
            values = [scenes_ref[date, band, tile_rows(i)].astype(jnp.float32) for band in range(bands)]
            out = []
            here = [label == g for g in range(REGIONS)]
            for value in (*values, 1.0):
                out += [sums[len(out) + g] + fold(jnp.where(here[g], value, 0.0)) for g in range(REGIONS)]
            return tuple(out)

        zero = jnp.zeros((TILE, cols), jnp.float32)
        sums = lax.fori_loop(0, tiles, gather, (zero,) * (REGIONS * per_region), unroll=min(tiles, 4))
        for i, total in enumerate(sums):
            sums_ref[date, i : i + 1] = jnp.sum(total, axis=0, keepdims=True)

    means = []
    for date in range(date_dev):
        totals = jnp.sum(sums_ref[date], axis=1, keepdims=True)
        counts = totals[bands * REGIONS :] + 1.0
        for band in range(bands):
            mean = totals[band * REGIONS : (band + 1) * REGIONS] / counts
            means.append([mean[g : g + 1] for g in range(REGIONS)])

    region = region_ref[...]
    row = lax.broadcasted_iota(jnp.int32, (TILE, cols), 0)
    half = TILE // 2
    for band in range(bands):
        anomalies = []
        for date in range(date_dev):
            mean = jnp.zeros((rows, cols), jnp.float32)
            for g in range(REGIONS):
                mean = jnp.where(region == g, jnp.broadcast_to(means[date * bands + band][g], (rows, cols)), mean)
            clear = mask_ref[date].astype(jnp.float32)
            anomalies.append(clear * (scenes_ref[date, band].astype(jnp.float32) - mean))
        per_slab = bands * plan.shared
        for slab in range(plan.slabs):
            if plan.compact:
                size = plan.slab_rows
                blocks = [anomaly[slab * size : (slab + 1) * size] for anomaly in anomalies]
                edge = size if slab == 0 else size - TILE
                wanted = row < half if slab == 0 else row >= half
                other = pltpu.roll(anomalies[1][edge : edge + TILE], half, 0)
                blocks.append(jnp.where(wanted, anomalies[0][edge : edge + TILE], other))
            else:
                first = plan.start(slab * per_slab)
                blocks = [anomaly[first : first + plan.window] for anomaly in anomalies]
            offset = 0
            for block in blocks:
                block = block.astype(jnp.bfloat16)
                for target in range(slab * per_slab + band, (slab + 1) * per_slab, bands):
                    send_ref[target, offset : offset + block.shape[0]] = block
                offset += block.shape[0]


def diffuse_kernel(plan, got_ref, region_ref, gram_ref, field_ref, other_ref, wide_ref, land_ref, row_ref, col_ref, turn_ref):
    window, dates, fine, wire = plan.window, plan.dates, plan.fine, plan.wire
    cols = got_ref.shape[-1]
    me = lax.axis_index("dates")
    start = plan.start(me)
    slab = plan.slab(me)
    own_first = slab * plan.slab_rows - start

    land_ref[: plan.rows] = (region_ref[...] > 0).astype(jnp.float32)
    here = land_ref[pl.ds(start, window)]
    row = lax.broadcasted_iota(jnp.int32, (window, cols), 0)
    col = lax.broadcasted_iota(jnp.int32, (window, cols), 1)
    above = jnp.where(row > 0, pltpu.roll(here, 1, 0), 0.0)
    right = jnp.where(col < cols - 1, pltpu.roll(here, cols - 1, 1), 0.0)
    row_weight = lam_space * here * above
    col_weight = lam_space * here * right
    for r in range(window):
        row_ref[r * TILE : (r + 1) * TILE] = jnp.broadcast_to(row_weight[r : r + 1], (TILE, cols))
        col_ref[r * TILE : (r + 1) * TILE] = jnp.broadcast_to(col_weight[r : r + 1], (TILE, cols))
    row_ref[window * TILE :] = jnp.zeros((TILE, cols), jnp.float32)
    for ref in (field_ref, other_ref):
        ref[window * dates :] = jnp.zeros((dates, cols), jnp.float32)
    sublane = lax.broadcasted_iota(jnp.int32, (TILE, cols), 0)
    last_weight = jnp.where(sublane < TILE - 1, lam_time, 0.0)
    source = lax.broadcasted_iota(jnp.int32, (cols, cols), 0)
    target = lax.broadcasted_iota(jnp.int32, (cols, cols), 1)
    same = (source == target).astype(jnp.float32)
    onward = ((source == target + 1).astype(jnp.float32) - same).astype(jnp.bfloat16)
    inflow = (same - (source + 1 == target).astype(jnp.float32)).astype(jnp.bfloat16)

    def widen(device, carry):
        wide_ref[pl.ds(pl.multiple_of(device * wire, TILE), wire)] = got_ref[device].astype(jnp.float32)
        return carry

    lax.fori_loop(0, plan.devices, widen, 0, unroll=min(plan.devices, 16))
    old_ref, new_ref = (field_ref, other_ref) if STEPS % 2 == 0 else (other_ref, field_ref)
    stride = fine // plan.date_dev * wire

    def place(r, first, f):
        from_row = f // plan.date_dev * wire + first
        old_ref[pl.ds(pl.multiple_of(r * dates + f * TILE, TILE), TILE)] = wide_ref[pl.ds(from_row, TILE, stride=stride)]

    for f in range(fine):
        date = f % plan.date_dev
        if plan.compact:
            halo = 2 * plan.slab_rows + STEPS * jnp.where(slab == 0, date, 1 - date)
            halo_row = jnp.where(slab == 0, plan.slab_rows, 0)
            for i in range(plan.slab_rows):
                place(own_first + i, date * plan.slab_rows + i, f)
            for i in range(STEPS):
                place(halo_row + i, halo + i, f)
        else:
            for i in range(window):
                place(i, date * window + i, f)

    chunk = max(1, 256 // dates)

    for step in range(STEPS):
        if plan.compact:
            base, count = jnp.where(slab == 0, 0, step + 1), window - step - 1
        else:
            base, count = 0, window

        def rows(r, n):
            return pl.ds(pl.multiple_of(r * dates, TILE), n * dates)

        def weights(ref, r, n):
            parts = []
            for i in range(n):
                parts += [ref[pl.ds(pl.multiple_of((r + i) * TILE, TILE), TILE)]] * fine
            return jnp.concatenate(parts, axis=0)

        def advance(r, n, row_in):
            current, following = old_ref[rows(r, n)], old_ref[rows(r + 1, n)]
            difference = jnp.dot(current.astype(jnp.bfloat16), onward, preferred_element_type=jnp.float32)
            col_flux = weights(col_ref, r, n).astype(jnp.bfloat16) * phi(difference.astype(jnp.bfloat16))
            row_flux = weights(row_ref, r + 1, n) * phi(following - current)
            if n > 1:
                row_before = jnp.concatenate([row_in, row_flux[:-dates]], axis=0)
            else:
                row_before = row_in
            date_change = []
            for i in range(n):
                x = current[i * dates : (i + 1) * dates]
                later = jnp.concatenate([x[TILE:], pltpu.roll(x[:TILE], TILE - 1, 0)], axis=0)
                flux = phi(later - x)
                flux = jnp.concatenate([lam_time * flux[:-TILE], last_weight * flux[-TILE:]], axis=0)
                date_change.append(flux - jnp.concatenate([pltpu.roll(flux[-TILE:], 1, 0), flux[:-TILE]], axis=0))
            new_ref[rows(r, n)] = (
                current
                + (row_flux - row_before)
                + jnp.dot(col_flux, inflow, preferred_element_type=jnp.float32)
                + (date_change[0] if n == 1 else jnp.concatenate(date_change, axis=0))
            )
            return row_flux[-dates:]

        before = old_ref[rows(jnp.maximum(base - 1, 0), 1)]
        row_in = weights(row_ref, base, 1) * phi(old_ref[rows(base, 1)] - before)
        full = count // chunk
        row_in = lax.fori_loop(
            0, full, lambda k, carry: advance(base + k * chunk, chunk, carry), row_in, unroll=min(full, UNROLL)
        )
        if count % chunk:
            advance(base + full * chunk, count % chunk, row_in)
        old_ref, new_ref = new_ref, old_ref

    def gram_rows(i, total):
        pair = [
            field_ref[pl.ds(pl.multiple_of((own_first + 2 * i + j) * dates, TILE), dates)].astype(jnp.bfloat16)
            for j in range(2)
        ]
        both = jnp.concatenate(pair, axis=1)
        return total + lax.dot_general(both, both, (((1,), (1,)), ((), ())), preferred_element_type=jnp.float32)

    gram = lax.fori_loop(
        0, plan.slab_rows // 2, gram_rows, jnp.zeros((dates, dates), jnp.float32), unroll=min(8, plan.slab_rows // 2)
    )
    width = turn_ref.shape[1]
    for last in (False, True):
        for block in range(dates // width):
            part = gram[:, block * width : (block + 1) * width]
            for f in range(fine):
                turn_ref[pl.ds(block * dates + f, TILE, stride=fine)] = part[f * TILE : (f + 1) * TILE]
            if last:
                gram_ref[:, block * width : (block + 1) * width] = turn_ref[block * dates : (block + 1) * dates]
        if not last:
            gram = jnp.concatenate(
                [turn_ref[block * dates : (block + 1) * dates].T for block in range(dates // width)], axis=0
            )


def share_kernel(plan, field_ref, message_ref, rest_ref):
    dates, fine, own = plan.dates, plan.fine, plan.own_rows
    me = lax.axis_index("dates")
    place = me % plan.bands
    plane_first = (me // plan.bands) * plan.plane_rows - plan.start(me)

    def share(t, carry):
        from_row = t % fine * TILE + t // fine
        for ref, slot, other in (
            (message_ref, t, 3), (message_ref, dates + t, 2), (rest_ref, t, 0), (rest_ref, dates + t, 1)
        ):
            first = (plane_first + (place ^ other) * own) * dates
            ref[slot] = field_ref[pl.ds(first + from_row, own, stride=dates)].astype(jnp.bfloat16)
        return carry

    lax.fori_loop(0, dates, share, 0, unroll=8)


def relay_kernel(plan, got_ref, rest_ref, message_ref):
    dates = plan.dates
    message_ref[:dates] = rest_ref[dates:]
    message_ref[dates:] = got_ref[dates:]


def sum_kernel(scale, mine_ref, other_ref, sim_ref):
    sim_ref[...] = (mine_ref[...] + other_ref[...]) * scale


def finish_kernel(plan, rest_ref, first_ref, second_ref, sim_ref, out_hbm, sim_hbm, sems):
    dates = plan.dates
    place = lax.axis_index("dates") % plan.bands
    head, tail = pl.ds(0, dates), pl.ds(dates, dates)
    copies = [
        pltpu.make_async_copy(source.at[part], out_hbm.at[:, place ^ other], sems.at[i])
        for i, (source, part, other) in enumerate(
            ((rest_ref, head, 0), (first_ref, head, 3), (second_ref, head, 1), (second_ref, tail, 2))
        )
    ]
    for copy in copies:
        copy.start()
    copies.append(pltpu.make_async_copy(sim_ref, sim_hbm, sems.at[4]))
    copies[-1].start()
    for copy in copies:
        copy.wait()


def add_kernel(gram_ref, got_ref, message_ref, sum_ref):
    sum_ref[...] = gram_ref[...] + got_ref[...]


def swap(x, bits):
    count = lax.axis_size("dates")
    return lax.ppermute(x, "dates", [(i, i ^ bits) for i in range(count)])


def local(scenes, cloud_mask, region):
    date_dev, bands, rows, cols = scenes.shape
    devices = lax.axis_size("dates")
    plan = Plan(devices, date_dev, bands, rows)
    dates, own = plan.dates, plan.own_rows
    me = lax.axis_index("dates")
    vmem = pl.BlockSpec(memory_space=pltpu.VMEM)
    hbm = pl.BlockSpec(memory_space=pltpu.MemorySpace.HBM)
    params = pltpu.CompilerParams(vmem_limit_bytes=LIMIT)
    moved = dates * bands * own * cols
    small = pl.CostEstimate(flops=moved, bytes_accessed=4 * moved, transcendentals=0)

    def shape(*sizes, dtype=jnp.bfloat16):
        return jax.ShapeDtypeStruct(sizes, dtype)

    send = pl.pallas_call(
        functools.partial(anomaly_kernel, plan),
        out_shape=shape(devices, plan.wire, cols),
        in_specs=[hbm] * 3,
        out_specs=vmem,
        scratch_shapes=[
            pltpu.VMEM(scenes.shape, scenes.dtype),
            pltpu.VMEM(cloud_mask.shape, cloud_mask.dtype),
            pltpu.VMEM(region.shape, region.dtype),
            pltpu.VMEM((date_dev, REGIONS * (bands + 1), cols), jnp.float32),
            pltpu.SemaphoreType.DMA((3,)),
        ],
        compiler_params=params,
    )(*(pltpu.with_memory_space_constraint(x, pltpu.MemorySpace.HBM) for x in (scenes, cloud_mask, region)))
    got = lax.all_to_all(send, "dates", split_axis=0, concat_axis=0, tiled=True)
    gram, field = pl.pallas_call(
        functools.partial(diffuse_kernel, plan),
        out_shape=(shape(dates, dates, dtype=jnp.float32), shape(dates * (plan.window + 1), cols, dtype=jnp.float32)),
        in_specs=[vmem] * 2,
        out_specs=(vmem,) * 2,
        scratch_shapes=[
            pltpu.VMEM((dates * (plan.window + 1), cols), jnp.float32),
            pltpu.VMEM((devices * plan.wire, cols), jnp.float32),
            pltpu.VMEM((rows, cols), jnp.float32),
            pltpu.VMEM(((plan.window + 1) * TILE, cols), jnp.float32),
            pltpu.VMEM((plan.window * TILE, cols), jnp.float32),
            pltpu.VMEM((dates * max(1, dates // 128), min(dates, 128)), jnp.float32),
        ],
        compiler_params=params,
    )(got, region)
    first_gram = swap(gram, 1)
    rows_shape = shape(2 * dates, own, cols)
    message, rest = pl.pallas_call(
        functools.partial(share_kernel, plan),
        out_shape=(rows_shape, rows_shape),
        in_specs=[vmem],
        out_specs=(vmem,) * 2,
        compiler_params=params,
        cost_estimate=small,
    )(field)
    first = swap(message, 3)
    gram = pl.pallas_call(
        add_kernel,
        out_shape=shape(dates, dates, dtype=jnp.float32),
        in_specs=[vmem] * 3,
        out_specs=vmem,
        compiler_params=params,
    )(gram, first_gram, message)
    gram = gram + swap(gram, 3)

    bit = bands * plan.shared
    while 2 * bit < devices:
        gram = gram + swap(gram, bit + 1)
        bit *= 2

    def rows_of(index):
        return lax.dynamic_slice_in_dim(gram, index * date_dev, date_dev, 0)

    mine = rows_of(me)
    other = swap(rows_of(me ^ (bit + 1)), bit + 1) if bit < devices else jnp.zeros_like(mine)
    message = pl.pallas_call(
        functools.partial(relay_kernel, plan),
        out_shape=rows_shape,
        in_specs=[vmem] * 2,
        out_specs=vmem,
        compiler_params=params,
        cost_estimate=small,
    )(first, rest)
    second = swap(message, 1)
    similarity = pl.pallas_call(
        functools.partial(sum_kernel, 1.0 / (bands * rows * cols)),
        out_shape=shape(date_dev, dates, dtype=jnp.float32),
        in_specs=[vmem] * 2,
        out_specs=vmem,
        compiler_params=params,
        cost_estimate=pl.CostEstimate(flops=HEAVY, bytes_accessed=HEAVY // 100, transcendentals=0),
    )(mine, other)
    return pl.pallas_call(
        functools.partial(finish_kernel, plan),
        out_shape=(shape(dates, bands, own, cols), shape(date_dev, dates, dtype=jnp.float32)),
        in_specs=[vmem] * 4,
        out_specs=(hbm,) * 2,
        scratch_shapes=[pltpu.SemaphoreType.DMA((5,))],
        compiler_params=params,
        cost_estimate=small,
    )(rest, first, second, similarity)


def solution(mesh):
    in_specs = (
        P(("groups", "dates"), None, None, None),
        P(("groups", "dates"), None, None),
        P("groups", None),
    )
    out_specs = (P("groups", None, "dates", None), P(("groups", "dates"), None))
    return jax.shard_map(local, mesh=mesh, in_specs=in_specs, out_specs=out_specs, check_vma=False)
```

```python
import functools

import jax
import jax.numpy as jnp
from jax import lax
from jax.experimental import pallas as pl
from jax.experimental.pallas import tpu as pltpu
from jax.sharding import PartitionSpec as P

REGIONS = 8
STEPS = 4
TILE = 8
SHARED = 2
UNROLL = 8

lam_space = 0.2
lam_time = 0.08

LIMIT = 48 * 1024 * 1024
HEAVY = 10**10


def phi(difference):
    return difference / (1.0 + difference * difference)


class Plan:
    def __init__(self, devices, date_dev, bands, rows):
        self.devices, self.date_dev, self.bands, self.rows = devices, date_dev, bands, rows
        self.dates = devices * date_dev
        planes = devices // bands
        self.shared = min(SHARED, planes)
        self.slabs = planes // self.shared
        self.plane_rows = rows // planes
        self.own_rows = rows // devices
        self.slab_rows = rows // self.slabs
        self.window = self.slab_rows + STEPS * min(self.slabs - 1, 2)
        self.fine = self.dates // TILE
        self.compact = self.slabs == 2 and date_dev == 2
        self.wire = 2 * self.slab_rows + TILE if self.compact else date_dev * self.window

    def slab(self, index):
        return index // (self.bands * self.shared)

    def start(self, index):
        first = self.slab(index) * self.slab_rows - STEPS
        last = self.rows - self.window
        if isinstance(index, int):
            return min(max(first, 0), last)
        return jnp.clip(first, 0, last)


def anomaly_kernel(plan, scenes_hbm, mask_hbm, region_hbm, send_ref, scenes_ref, mask_ref, region_ref, sums_ref, sems):
    date_dev, bands, rows, cols = scenes_ref.shape
    copies = [
        pltpu.make_async_copy(source, target, sems.at[i])
        for i, (source, target) in enumerate(
            ((scenes_hbm, scenes_ref), (mask_hbm, mask_ref), (region_hbm, region_ref))
        )
    ]
    for copy in copies:
        copy.start()
    for copy in copies:
        copy.wait()

    step = 2 * TILE
    tiles = rows // step
    per_region = bands + 1

    def tile_rows(i):
        return pl.ds(pl.multiple_of(i * step, step), step)

    for date in range(date_dev):

        def fold(x):
            return x[:TILE] + x[TILE:]

        def gather(i, sums):
            clear = mask_ref[date, tile_rows(i)] > 0
            label = jnp.where(clear, region_ref[tile_rows(i)], -1)
            values = [scenes_ref[date, band, tile_rows(i)].astype(jnp.float32) for band in range(bands)]
            out = []
            here = [label == g for g in range(REGIONS)]
            for value in (*values, 1.0):
                out += [sums[len(out) + g] + fold(jnp.where(here[g], value, 0.0)) for g in range(REGIONS)]
            return tuple(out)

        zero = jnp.zeros((TILE, cols), jnp.float32)
        sums = lax.fori_loop(0, tiles, gather, (zero,) * (REGIONS * per_region), unroll=min(tiles, 4))
        for i, total in enumerate(sums):
            sums_ref[date, i : i + 1] = jnp.sum(total, axis=0, keepdims=True)

    means = []
    for date in range(date_dev):
        totals = jnp.sum(sums_ref[date], axis=1, keepdims=True)
        counts = totals[bands * REGIONS :] + 1.0
        for band in range(bands):
            mean = totals[band * REGIONS : (band + 1) * REGIONS] / counts
            means.append([mean[g : g + 1] for g in range(REGIONS)])

    region = region_ref[...]
    row = lax.broadcasted_iota(jnp.int32, (TILE, cols), 0)
    half = TILE // 2
    for band in range(bands):
        anomalies = []
        for date in range(date_dev):
            mean = jnp.zeros((rows, cols), jnp.float32)
            for g in range(REGIONS):
                mean = jnp.where(region == g, jnp.broadcast_to(means[date * bands + band][g], (rows, cols)), mean)
            clear = mask_ref[date].astype(jnp.float32)
            anomalies.append(clear * (scenes_ref[date, band].astype(jnp.float32) - mean))
        per_slab = bands * plan.shared
        for slab in range(plan.slabs):
            if plan.compact:
                size = plan.slab_rows
                blocks = [anomaly[slab * size : (slab + 1) * size] for anomaly in anomalies]
                edge = size if slab == 0 else size - TILE
                wanted = row < half if slab == 0 else row >= half
                other = pltpu.roll(anomalies[1][edge : edge + TILE], half, 0)
                blocks.append(jnp.where(wanted, anomalies[0][edge : edge + TILE], other))
            else:
                first = plan.start(slab * per_slab)
                blocks = [anomaly[first : first + plan.window] for anomaly in anomalies]
            offset = 0
            for block in blocks:
                block = block.astype(jnp.bfloat16)
                for target in range(slab * per_slab + band, (slab + 1) * per_slab, bands):
                    send_ref[target, offset : offset + block.shape[0]] = block
                offset += block.shape[0]


def diffuse_kernel(plan, got_ref, region_ref, gram_ref, field_ref, other_ref, wide_ref, land_ref, row_ref, col_ref, turn_ref):
    window, dates, fine, wire = plan.window, plan.dates, plan.fine, plan.wire
    cols = got_ref.shape[-1]
    me = lax.axis_index("dates")
    start = plan.start(me)
    slab = plan.slab(me)
    own_first = slab * plan.slab_rows - start

    land_ref[: plan.rows] = (region_ref[...] > 0).astype(jnp.float32)
    here = land_ref[pl.ds(start, window)]
    row = lax.broadcasted_iota(jnp.int32, (window, cols), 0)
    col = lax.broadcasted_iota(jnp.int32, (window, cols), 1)
    above = jnp.where(row > 0, pltpu.roll(here, 1, 0), 0.0)
    right = jnp.where(col < cols - 1, pltpu.roll(here, cols - 1, 1), 0.0)
    row_weight = lam_space * here * above
    col_weight = lam_space * here * right
    for r in range(window):
        row_ref[r * TILE : (r + 1) * TILE] = jnp.broadcast_to(row_weight[r : r + 1], (TILE, cols))
        col_ref[r * TILE : (r + 1) * TILE] = jnp.broadcast_to(col_weight[r : r + 1], (TILE, cols))
    row_ref[window * TILE :] = jnp.zeros((TILE, cols), jnp.float32)
    for ref in (field_ref, other_ref):
        ref[window * dates :] = jnp.zeros((dates, cols), jnp.float32)
    sublane = lax.broadcasted_iota(jnp.int32, (TILE, cols), 0)
    last_weight = jnp.where(sublane < TILE - 1, lam_time, 0.0)
    source = lax.broadcasted_iota(jnp.int32, (cols, cols), 0)
    target = lax.broadcasted_iota(jnp.int32, (cols, cols), 1)
    same = (source == target).astype(jnp.float32)
    onward = ((source == target + 1).astype(jnp.float32) - same).astype(jnp.bfloat16)
    inflow = (same - (source + 1 == target).astype(jnp.float32)).astype(jnp.bfloat16)

    def widen(device, carry):
        wide_ref[pl.ds(pl.multiple_of(device * wire, TILE), wire)] = got_ref[device].astype(jnp.float32)
        return carry

    lax.fori_loop(0, plan.devices, widen, 0, unroll=min(plan.devices, 16))
    old_ref, new_ref = (field_ref, other_ref) if STEPS % 2 == 0 else (other_ref, field_ref)
    stride = fine // plan.date_dev * wire

    def place(r, first, f):
        from_row = f // plan.date_dev * wire + first
        old_ref[pl.ds(pl.multiple_of(r * dates + f * TILE, TILE), TILE)] = wide_ref[pl.ds(from_row, TILE, stride=stride)]

    for f in range(fine):
        date = f % plan.date_dev
        if plan.compact:
            halo = 2 * plan.slab_rows + STEPS * jnp.where(slab == 0, date, 1 - date)
            halo_row = jnp.where(slab == 0, plan.slab_rows, 0)
            for i in range(plan.slab_rows):
                place(own_first + i, date * plan.slab_rows + i, f)
            for i in range(STEPS):
                place(halo_row + i, halo + i, f)
        else:
            for i in range(window):
                place(i, date * window + i, f)

    chunk = max(1, 384 // dates)

    for step in range(STEPS):
        if plan.compact:
            base, count = jnp.where(slab == 0, 0, step + 1), window - step - 1
        else:
            base, count = 0, window

        def rows(r, n):
            return pl.ds(pl.multiple_of(r * dates, TILE), n * dates)

        def weights(ref, r, n):
            parts = []
            for i in range(n):
                parts += [ref[pl.ds(pl.multiple_of((r + i) * TILE, TILE), TILE)]] * fine
            return jnp.concatenate(parts, axis=0)

        def advance(r, n, row_in):
            current, following = old_ref[rows(r, n)], old_ref[rows(r + 1, n)]
            difference = jnp.dot(current.astype(jnp.bfloat16), onward, preferred_element_type=jnp.float32)
            col_flux = (weights(col_ref, r, n) * phi(difference)).astype(jnp.bfloat16)
            row_flux = weights(row_ref, r + 1, n) * phi(following - current)
            if n > 1:
                row_before = jnp.concatenate([row_in, row_flux[:-dates]], axis=0)
            else:
                row_before = row_in
            date_change = []
            for i in range(n):
                x = current[i * dates : (i + 1) * dates]
                later = jnp.concatenate([x[TILE:], pltpu.roll(x[:TILE], TILE - 1, 0)], axis=0)
                flux = phi(later - x)
                flux = jnp.concatenate([lam_time * flux[:-TILE], last_weight * flux[-TILE:]], axis=0)
                date_change.append(flux - jnp.concatenate([pltpu.roll(flux[-TILE:], 1, 0), flux[:-TILE]], axis=0))
            new_ref[rows(r, n)] = (
                current
                + (row_flux - row_before)
                + jnp.dot(col_flux, inflow, preferred_element_type=jnp.float32)
                + (date_change[0] if n == 1 else jnp.concatenate(date_change, axis=0))
            )
            return row_flux[-dates:]

        before = old_ref[rows(jnp.maximum(base - 1, 0), 1)]
        row_in = weights(row_ref, base, 1) * phi(old_ref[rows(base, 1)] - before)
        full = count // chunk
        row_in = lax.fori_loop(
            0, full, lambda k, carry: advance(base + k * chunk, chunk, carry), row_in, unroll=min(full, UNROLL)
        )
        if count % chunk:
            advance(base + full * chunk, count % chunk, row_in)
        old_ref, new_ref = new_ref, old_ref

    def gram_rows(i, total):
        pair = [
            field_ref[pl.ds(pl.multiple_of((own_first + 2 * i + j) * dates, TILE), dates)].astype(jnp.bfloat16)
            for j in range(2)
        ]
        both = jnp.concatenate(pair, axis=1)
        return total + lax.dot_general(both, both, (((1,), (1,)), ((), ())), preferred_element_type=jnp.float32)

    gram = lax.fori_loop(
        0, plan.slab_rows // 2, gram_rows, jnp.zeros((dates, dates), jnp.float32), unroll=min(8, plan.slab_rows // 2)
    )
    width = turn_ref.shape[1]
    for last in (False, True):
        for block in range(dates // width):
            part = gram[:, block * width : (block + 1) * width]
            for f in range(fine):
                turn_ref[pl.ds(block * dates + f, TILE, stride=fine)] = part[f * TILE : (f + 1) * TILE]
            if last:
                gram_ref[:, block * width : (block + 1) * width] = turn_ref[block * dates : (block + 1) * dates]
        if not last:
            gram = jnp.concatenate(
                [turn_ref[block * dates : (block + 1) * dates].T for block in range(dates // width)], axis=0
            )


def share_kernel(plan, field_ref, message_ref, rest_ref):
    dates, fine, own = plan.dates, plan.fine, plan.own_rows
    me = lax.axis_index("dates")
    place = me % plan.bands
    plane_first = (me // plan.bands) * plan.plane_rows - plan.start(me)

    def share(t, carry):
        from_row = t % fine * TILE + t // fine
        for ref, slot, other in (
            (message_ref, t, 3), (message_ref, dates + t, 2), (rest_ref, t, 0), (rest_ref, dates + t, 1)
        ):
            first = (plane_first + (place ^ other) * own) * dates
            ref[slot] = field_ref[pl.ds(first + from_row, own, stride=dates)].astype(jnp.bfloat16)
        return carry

    lax.fori_loop(0, dates, share, 0, unroll=8)


def relay_kernel(plan, got_ref, rest_ref, message_ref):
    dates = plan.dates
    message_ref[:dates] = rest_ref[dates:]
    message_ref[dates:] = got_ref[dates:]


def sum_kernel(scale, mine_ref, other_ref, sim_ref):
    sim_ref[...] = (mine_ref[...] + other_ref[...]) * scale


def finish_kernel(plan, rest_ref, first_ref, second_ref, sim_ref, out_hbm, sim_hbm, sems):
    dates = plan.dates
    place = lax.axis_index("dates") % plan.bands
    head, tail = pl.ds(0, dates), pl.ds(dates, dates)
    copies = [
        pltpu.make_async_copy(source.at[part], out_hbm.at[:, place ^ other], sems.at[i])
        for i, (source, part, other) in enumerate(
            ((rest_ref, head, 0), (first_ref, head, 3), (second_ref, head, 1), (second_ref, tail, 2))
        )
    ]
    for copy in copies:
        copy.start()
    copies.append(pltpu.make_async_copy(sim_ref, sim_hbm, sems.at[4]))
    copies[-1].start()
    for copy in copies:
        copy.wait()


def add_kernel(gram_ref, got_ref, message_ref, sum_ref):
    sum_ref[...] = gram_ref[...] + got_ref[...]


def swap(x, bits):
    count = lax.axis_size("dates")
    return lax.ppermute(x, "dates", [(i, i ^ bits) for i in range(count)])


def local(scenes, cloud_mask, region):
    date_dev, bands, rows, cols = scenes.shape
    devices = lax.axis_size("dates")
    plan = Plan(devices, date_dev, bands, rows)
    dates, own = plan.dates, plan.own_rows
    me = lax.axis_index("dates")
    vmem = pl.BlockSpec(memory_space=pltpu.VMEM)
    hbm = pl.BlockSpec(memory_space=pltpu.MemorySpace.HBM)
    params = pltpu.CompilerParams(vmem_limit_bytes=LIMIT)
    moved = dates * bands * own * cols
    small = pl.CostEstimate(flops=moved, bytes_accessed=4 * moved, transcendentals=0)

    def shape(*sizes, dtype=jnp.bfloat16):
        return jax.ShapeDtypeStruct(sizes, dtype)

    send = pl.pallas_call(
        functools.partial(anomaly_kernel, plan),
        out_shape=shape(devices, plan.wire, cols),
        in_specs=[hbm] * 3,
        out_specs=vmem,
        scratch_shapes=[
            pltpu.VMEM(scenes.shape, scenes.dtype),
            pltpu.VMEM(cloud_mask.shape, cloud_mask.dtype),
            pltpu.VMEM(region.shape, region.dtype),
            pltpu.VMEM((date_dev, REGIONS * (bands + 1), cols), jnp.float32),
            pltpu.SemaphoreType.DMA((3,)),
        ],
        compiler_params=params,
    )(*(pltpu.with_memory_space_constraint(x, pltpu.MemorySpace.HBM) for x in (scenes, cloud_mask, region)))
    got = lax.all_to_all(send, "dates", split_axis=0, concat_axis=0, tiled=True)
    gram, field = pl.pallas_call(
        functools.partial(diffuse_kernel, plan),
        out_shape=(shape(dates, dates, dtype=jnp.float32), shape(dates * (plan.window + 1), cols, dtype=jnp.float32)),
        in_specs=[vmem] * 2,
        out_specs=(vmem,) * 2,
        scratch_shapes=[
            pltpu.VMEM((dates * (plan.window + 1), cols), jnp.float32),
            pltpu.VMEM((devices * plan.wire, cols), jnp.float32),
            pltpu.VMEM((rows, cols), jnp.float32),
            pltpu.VMEM(((plan.window + 1) * TILE, cols), jnp.float32),
            pltpu.VMEM((plan.window * TILE, cols), jnp.float32),
            pltpu.VMEM((dates * max(1, dates // 128), min(dates, 128)), jnp.float32),
        ],
        compiler_params=params,
    )(got, region)
    first_gram = swap(gram, 1)
    rows_shape = shape(2 * dates, own, cols)
    message, rest = pl.pallas_call(
        functools.partial(share_kernel, plan),
        out_shape=(rows_shape, rows_shape),
        in_specs=[vmem],
        out_specs=(vmem,) * 2,
        compiler_params=params,
        cost_estimate=small,
    )(field)
    first = swap(message, 3)
    gram = pl.pallas_call(
        add_kernel,
        out_shape=shape(dates, dates, dtype=jnp.float32),
        in_specs=[vmem] * 3,
        out_specs=vmem,
        compiler_params=params,
    )(gram, first_gram, message)
    gram = gram + swap(gram, 3)

    bit = bands * plan.shared
    while 2 * bit < devices:
        gram = gram + swap(gram, bit + 1)
        bit *= 2

    def rows_of(index):
        return lax.dynamic_slice_in_dim(gram, index * date_dev, date_dev, 0)

    mine = rows_of(me)
    other = swap(rows_of(me ^ (bit + 1)), bit + 1) if bit < devices else jnp.zeros_like(mine)
    message = pl.pallas_call(
        functools.partial(relay_kernel, plan),
        out_shape=rows_shape,
        in_specs=[vmem] * 2,
        out_specs=vmem,
        compiler_params=params,
        cost_estimate=small,
    )(first, rest)
    second = swap(message, 1)
    similarity = pl.pallas_call(
        functools.partial(sum_kernel, 1.0 / (bands * rows * cols)),
        out_shape=shape(date_dev, dates, dtype=jnp.float32),
        in_specs=[vmem] * 2,
        out_specs=vmem,
        compiler_params=params,
        cost_estimate=pl.CostEstimate(flops=HEAVY, bytes_accessed=HEAVY // 100, transcendentals=0),
    )(mine, other)
    return pl.pallas_call(
        functools.partial(finish_kernel, plan),
        out_shape=(shape(dates, bands, own, cols), shape(date_dev, dates, dtype=jnp.float32)),
        in_specs=[vmem] * 4,
        out_specs=(hbm,) * 2,
        scratch_shapes=[pltpu.SemaphoreType.DMA((5,))],
        compiler_params=params,
        cost_estimate=small,
    )(rest, first, second, similarity)


def solution(mesh):
    in_specs = (
        P(("groups", "dates"), None, None, None),
        P(("groups", "dates"), None, None),
        P("groups", None),
    )
    out_specs = (P("groups", None, "dates", None), P(("groups", "dates"), None))
    return jax.shard_map(local, mesh=mesh, in_specs=in_specs, out_specs=out_specs, check_vma=False)
```
